32 devices in a mesh: expert: 4 (over x, core), node: 8 (over z, y).
Axes of the slice: x: 2, y: 2, z: 4, core: 2. Of those that a mesh axis runs over, the one named last changes fastest.
Arguments:
- tokens: bfloat16 [2, 8192, 1024], P(None, ('expert', 'node')), may hold values from -6 to 6
- routing: int32 [2, 8192], P(None, ('expert', 'node')), may hold values from 0 to 3, as said below
- out_grad: bfloat16 [2, 8192, 512], P(None, ('expert', 'node')), may hold values from -6 to 6
- weights: float32 [8, 4, 1024, 512], P('node', 'expert'), may hold values from -5 to 5
- momentum: float32 [8, 4, 1024, 512], P('node', 'expert'), may hold values from -8 to 8
Outputs:
- new_weights: float32 [8, 4, 1024, 512], P('node', 'expert')
- new_momentum: float32 [8, 4, 1024, 512], P('node', 'expert')
- in_grad: bfloat16 [2, 8192, 1024], P(None, ('expert', 'node'))
The draws below stay inside these ranges and needn't reach their ends.
Inputs may be any that keep to these rules, and one draw needn't show every extreme that they name: `routing`: within each block of 256 rows of one round (the rows of one device), no expert is named more than 128 times; in every round each node has one expert that is named exactly 128 times in each of that node's blocks.
All inputs are finite; a program needn't handle non-finite values.
Results may differ from the reference program's by a relative error of at most 0.0065.
Values may be sent and summed in bfloat16 or wider, within the bound.
No kernel may reach another device: no remote copies, remote signals or barrier semaphores. Data moves between devices by JAX's collectives and lax.ppermute only.
A program may use at most 64 MiB of HBM per device.

```python
import math
import jax
import jax.numpy as jnp
from jax import lax

D = 1024
H = 512
TOK_DEV = 256
ROUNDS = 2
NS_STEPS = 3
EXPERTS = 4
CAP = 128
NODES = 8
TOKENS = 8192
N_EXPERT = 4


def draw_routing(key, part):
    blocks = TOKENS // TOK_DEV
    full_key, cut_key, order_key = jax.random.split(key, 3)
    full_pick = jax.random.randint(full_key, (ROUNDS, 1, NODES), 0, EXPERTS)
    full_pick = jnp.broadcast_to(full_pick, (ROUNDS, blocks // NODES, NODES)).reshape(ROUNDS, blocks, 1)
    spare_rows = TOK_DEV - CAP
    cut_points = jnp.sort(jax.random.randint(cut_key, (ROUNDS, blocks, EXPERTS - 2), 0, spare_rows + 1), axis=-1)
    upper_edges = jnp.concatenate([cut_points, jnp.full((ROUNDS, blocks, 1), spare_rows, jnp.int32)], axis=-1)
    places = jnp.arange(TOK_DEV, dtype=jnp.int32)
    beyond = places - CAP
    passed = jnp.sum((beyond[None, None, :, None] >= upper_edges[:, :, None, :]).astype(jnp.int32), axis=-1)
    others = (full_pick + 1 + passed) % EXPERTS
    labels = jnp.where(places[None, None, :] < CAP, full_pick, others)
    scores = jax.random.randint(order_key, (ROUNDS, blocks, TOK_DEV), 0, 1048576) * TOK_DEV + places[None, None, :]
    shuffle = jnp.argsort(scores, axis=-1)
    labels = jnp.take_along_axis(labels, shuffle, axis=-1)
    return labels.reshape(ROUNDS, TOKENS).astype(jnp.int32)


def draw_momentum(key, part):
    base_key = jax.random.fold_in(key, 0)
    values = jax.random.normal(base_key, (NODES, EXPERTS, D, H), jnp.float32)
    return jnp.clip(values, -8.0, 8.0)


def level_of(own_key, dims, cuts, low, top_value):
    def one(position, shards_of):
        heights = jax.random.uniform(jax.random.fold_in(jax.random.fold_in(own_key, 6), position), (shards_of,), jnp.float32, low / len(cuts), top_value / len(cuts))
        return jnp.repeat(jnp.exp(heights), dims[position] // shards_of).reshape((-1,) + (1,) * (len(dims) - position - 1))

    level = one(*cuts[0])
    for cut in cuts[1:]:
        level = level * one(*cut)
    return level


def scatter_about(key, shape, width, reach, pieces=(), kind=jnp.bfloat16):
    loudness = level_of(key, shape, pieces, -0.22, 0.18) if pieces else 1.0
    drawn = jax.random.normal(key, shape, jnp.float32) * width * loudness
    return jnp.minimum(jnp.maximum(drawn, -reach), reach).astype(kind)


def setup_inputs(seed: int = 0) -> dict:
    key_of = jax.random.split(jax.random.key(seed), 6)
    return {
        "tokens": scatter_about(key_of[0], (ROUNDS, TOKENS, D), 1.0, 6.0, ((1, 32),)),
        "routing": draw_routing(jax.random.fold_in(key_of[5], 71), 0),
        "out_grad": scatter_about(key_of[2], (ROUNDS, TOKENS, H), 1.0, 6.0, ((1, 32),)),
        "weights": scatter_about(key_of[3], (NODES, EXPERTS, D, H), 1.0, 5.0, ((0, 8), (1, 4)), jnp.float32),
        "momentum": draw_momentum(jax.random.fold_in(key_of[5], 71), 0),
    }


def rounded(value):
    return lax.optimization_barrier(value.astype(jnp.bfloat16))

def per_node(item):
    node_tokens, node_grads, node_routes, node_weight, node_moment = item
    factor = 1.0 / math.sqrt(D)
    step_size = 0.1 * math.sqrt(D)
    labels = jnp.arange(EXPERTS, dtype=jnp.int32)
    onehot = (node_routes[:, :, None] == labels[None, None, :]).astype(jnp.int32)
    slot_rank = lax.optimization_barrier(jnp.sum(onehot * (jnp.cumsum(onehot, axis=1) - 1), axis=-1))
    sources = jnp.arange(N_EXPERT, dtype=jnp.int32)[:, None]
    target = (node_routes * (N_EXPERT * CAP) + sources * CAP + slot_rank).reshape(-1).astype(jnp.int32)
    row_buffer = jnp.zeros((EXPERTS * N_EXPERT * CAP, D), jnp.bfloat16)
    row_buffer = row_buffer.at[target].set(node_tokens.reshape(-1, D)).reshape(EXPERTS, N_EXPERT * CAP, D)
    grad_buffer = jnp.zeros((EXPERTS * N_EXPERT * CAP, H), jnp.bfloat16)
    grad_buffer = grad_buffer.at[target].set(node_grads.reshape(-1, H)).reshape(EXPERTS, N_EXPERT * CAP, H)
    shaped = rounded(node_weight).astype(jnp.float32)
    preact = jnp.einsum('erd,edh->erh', row_buffer.astype(jnp.float32), shaped) * factor
    slopes = rounded(grad_buffer.astype(jnp.float32) * 2.0 * jnp.maximum(preact, 0.0))
    slope_wide = slopes.astype(jnp.float32)
    backward = rounded(jnp.einsum('erh,edh->erd', slope_wide, shaped) * factor)
    grad_w = jnp.einsum('erd,erh->edh', row_buffer.astype(jnp.float32), slope_wide) * factor
    row_grads = backward.reshape(-1, D)[target].reshape(N_EXPERT, TOK_DEV, D)
    moment = 0.9 * node_moment + grad_w
    frob_norm = jnp.sqrt(lax.optimization_barrier(jnp.sum(moment * moment, axis=(1, 2), keepdims=True)))
    orthog = rounded(moment / (frob_norm + 1e-07))
    for sweep in range(NS_STEPS):
        orth_wide = orthog.astype(jnp.float32)
        gram_matrix = rounded(jnp.einsum('edh,edk->ehk', orth_wide, orth_wide))
        gram_wide = gram_matrix.astype(jnp.float32)
        square = jnp.einsum('ehk,ekj->ehj', gram_wide, gram_wide)
        polynom = rounded(-4.775 * gram_wide + 2.0315 * square)
        orthog = rounded(3.4445 * orth_wide + jnp.einsum('edh,ehk->edk', orth_wide, polynom.astype(jnp.float32)))
    stepped = node_weight - step_size * orthog.astype(jnp.float32)
    return (stepped, moment, row_grads)

def reference(tokens, routing, out_grad, weights, momentum):
    weight = weights
    moment = momentum
    in_grads = []
    for round_index in range(ROUNDS):
        node_tokens = tokens[round_index].reshape(N_EXPERT, NODES, TOK_DEV, D).transpose(1, 0, 2, 3)
        node_grads = out_grad[round_index].reshape(N_EXPERT, NODES, TOK_DEV, H).transpose(1, 0, 2, 3)
        node_routes = routing[round_index].reshape(N_EXPERT, NODES, TOK_DEV).transpose(1, 0, 2)
        stepped, moment, row_grads = lax.map(per_node, (node_tokens, node_grads, node_routes, weight, moment))
        in_grads.append(row_grads.transpose(1, 0, 2, 3).reshape(TOKENS, D))
        shared = rounded(stepped).astype(jnp.float32)
        neighbours = jnp.roll(shared, 1, axis=0) + jnp.roll(shared, -1, axis=0)
        neighbours = neighbours + jnp.roll(shared, 2, axis=0) + jnp.roll(shared, -2, axis=0)
        weight = 0.4 * stepped + 0.15 * neighbours
    return (weight, moment, jnp.stack(in_grads))
```

```python
import math

import jax
import jax.numpy as jnp
from jax import lax
from jax.experimental import pallas as pl
from jax.experimental.pallas import tpu as pltpu
from jax.sharding import PartitionSpec as P

ROUNDS = 2
NS_STEPS = 3
CHUNKS = 4
LEAD, LINEAR, QUADRATIC = 3.4445, -4.775, 2.0315
F32 = jnp.float32
BF16 = jnp.bfloat16
VMEM = pl.BlockSpec(memory_space=pltpu.VMEM)
SMEM = pl.BlockSpec(memory_space=pltpu.SMEM)
LIMIT = pltpu.CompilerParams(vmem_limit_bytes=56 << 20)


def shifted(block, axis, distance):
    count = lax.axis_size(axis)
    return lax.ppermute(block, axis, [((i - distance) % count, i) for i in range(count)])


def swapped(block, axis, bit):
    return lax.ppermute(block, axis, [(i, i ^ bit) for i in range(lax.axis_size(axis))])


def dot(a, b):
    return jnp.dot(a, b, preferred_element_type=F32)


def dot_first(a, b):
    return lax.dot_general(a, b, (((0,), (0,)), ((), ())), preferred_element_type=F32)


def dot_last(a, b):
    return lax.dot_general(a, b, (((1,), (1,)), ((), ())), preferred_element_type=F32)


def factors(gram):
    rest, lead = None, 1.0
    for sweep in range(NS_STEPS):
        wide = gram.astype(F32)
        polynom_wide = LINEAR * wide + QUADRATIC * dot(gram, gram)
        polynom = polynom_wide.astype(BF16)
        if sweep == 0:
            rest = polynom_wide
        else:
            rest = lead * polynom_wide + LEAD * rest + dot(rest.astype(BF16), polynom)
        lead = lead * LEAD
        if sweep < NS_STEPS - 1:
            half = (LEAD * wide + dot(gram, polynom)).astype(BF16)
            gram = (LEAD * half.astype(F32) + dot(half, polynom)).astype(BF16)
    return rest, lead


def round_kernel(blocks, place, refs):
    names = iter(refs)
    rows_refs = [next(names) for _ in range(blocks)]
    grad_refs = [next(names) for _ in range(blocks)]
    route, mine, weight, moment = (next(names) for _ in range(4))
    new_moment, slopes, stepped = (next(names) for _ in range(3))
    shares = [next(names) for _ in range(CHUNKS)]
    rows, shaped, moment_low = (next(names) for _ in range(3))
    depth, width = weight.shape
    count = rows_refs[0].shape[0]
    factor = 1.0 / math.sqrt(depth)
    step_size = 0.1 * math.sqrt(depth)
    shaped[...] = weight[...].astype(BF16)
    columns = route[...].T
    lanes = route.shape[1]
    for block in range(blocks):
        part = rows_refs[block][:, :depth]
        rows[pl.ds(block * count, count), :] = part
        pre = dot(part, shaped[...]) * factor
        for piece in range(count // lanes):
            index = block * (count // lanes) + piece
            keep = columns[:, index : index + 1] == mine[0]
            span = slice(piece * lanes, (piece + 1) * lanes)
            grads = grad_refs[block][span, place : place + width].astype(F32)
            slope = grads * 2.0 * jnp.maximum(pre[span, :], 0.0)
            slopes[pl.ds(index * lanes, lanes), :] = jnp.where(keep, slope, 0.0).astype(BF16)

    tile = min(256, depth)

    def accumulate(i, total):
        span = pl.ds(pl.multiple_of(i * tile, tile), tile)
        value = 0.9 * moment[span, :] + dot_first(rows[:, span], slopes[...]) * factor
        new_moment[span, :] = value
        moment_low[span, :] = value.astype(BF16)
        return total + jnp.sum(value * value, axis=0, keepdims=True)

    total = lax.fori_loop(0, depth // tile, accumulate, jnp.zeros((1, width), F32))
    scale = 1.0 / (jnp.sqrt(jnp.sum(total)) + 1e-07)
    gram = (dot_first(moment_low[...], moment_low[...]) * (scale * scale)).astype(BF16)
    rest, lead = factors(gram)
    rest = rest.astype(BF16)
    chunk = depth // CHUNKS
    for index in range(CHUNKS):
        span = pl.ds(index * chunk, chunk)
        low = moment_low[span, :]
        orthog = scale * (lead * low.astype(F32) + dot(low, rest))
        value = weight[span, :] - step_size * orthog
        stepped[span, :] = value
        shares[index][...] = value.astype(BF16)


def round_call(rows, grads, place, route, mine, weight, moment):
    depth, width = weight.shape
    blocks = len(rows)
    total = blocks * rows[0].shape[0]
    whole = jax.ShapeDtypeStruct((depth, width), F32)
    share = jax.ShapeDtypeStruct((depth // CHUNKS, width), BF16)
    result = pl.pallas_call(
        lambda *refs: round_kernel(blocks, place, refs),
        out_shape=[whole, jax.ShapeDtypeStruct((total, width), BF16), whole] + [share] * CHUNKS,
        in_specs=[VMEM] * (2 * blocks + 1) + [SMEM, VMEM, VMEM],
        out_specs=[VMEM] * (3 + CHUNKS),
        scratch_shapes=[
            pltpu.VMEM((total, depth), BF16),
            pltpu.VMEM((depth, width), BF16),
            pltpu.VMEM((depth, width), BF16),
        ],
        compiler_params=LIMIT,
        name="muon_round",
    )(*rows, *grads, route, mine, weight, moment)
    return result[0], result[1], result[2], result[3:]


def backward_kernel(slopes, weight, out):
    depth = weight.shape[0]
    factor = 1.0 / math.sqrt(depth)
    shaped = weight[...].astype(BF16)
    count = out.shape[1]
    for block in range(out.shape[0]):
        part = slopes[pl.ds(block * count, count), :]
        out[block] = (dot_last(part, shaped) * factor).astype(BF16)


def backward_call(slopes, weight, blocks):
    depth = weight.shape[0]
    return pl.pallas_call(
        backward_kernel,
        out_shape=jax.ShapeDtypeStruct((blocks, slopes.shape[0] // blocks, depth), BF16),
        in_specs=[VMEM, VMEM],
        out_specs=VMEM,
        compiler_params=LIMIT,
        name="row_gradients",
    )(slopes, weight)


def combine_kernel(stepped, left, right, near, *rest):
    out = rest[-1]
    total = left[...].astype(F32) + right[...].astype(F32) + near[...].astype(F32)
    out[...] = 0.4 * stepped[...] + 0.15 * total


def combine_call(index, stepped, left, right, near, buffer):
    chunk, width = left.shape
    place = pl.BlockSpec((chunk, width), lambda i: (index, 0))
    whole = pl.BlockSpec((chunk, width), lambda i: (0, 0))
    extra = [] if buffer is None else [buffer]
    return pl.pallas_call(
        combine_kernel,
        grid=(1,),
        out_shape=jax.ShapeDtypeStruct(stepped.shape, F32),
        in_specs=[place, whole, whole, whole] + [pl.BlockSpec(memory_space=pl.ANY)] * len(extra),
        out_specs=place,
        input_output_aliases={4: 0} if extra else {},
        compiler_params=pltpu.CompilerParams(vmem_limit_bytes=16 << 20),
        name="average",
    )(stepped, left, right, near, *extra)


def on_device(tokens, routing, out_grad, weights, momentum):
    experts = lax.axis_size("expert")
    bits = []
    bit = experts // 2
    while bit:
        bits.append(bit)
        bit //= 2
    weight = weights[0, 0]
    moment = momentum[0, 0]
    width = weight.shape[1]
    mine = lax.axis_index("expert").astype(jnp.int32).reshape(1)
    even = lax.axis_index("node") % 2 == 0

    def gathered(own):
        held = [own]
        for bit in bits:
            held = held + [swapped(item, "expert", bit) for item in held]
        return held

    def returned(parts):
        for bit in reversed(bits):
            half = parts.shape[0] // 2
            parts = parts[:half] + swapped(parts[half:], "expert", bit)
        return parts[0]

    routes = gathered(routing)
    rows = [gathered(tokens[0])]
    grads = [gathered(out_grad[0])]
    places = [0]
    packed = jnp.concatenate([tokens[1], out_grad[1]], axis=1)
    packed, _ = lax.optimization_barrier((packed, rows[0][1]))
    later = gathered(packed)
    rows.append(later)
    grads.append(later)
    places.append(tokens.shape[2])
    in_grads = []
    for index in range(ROUNDS):
        route = jnp.concatenate([item[index] for item in routes]).reshape(-1, 128)
        moment, slopes, stepped, shares = round_call(
            rows[index], grads[index], places[index], route, mine, weight, moment
        )
        partial_rows = backward_call(slopes, weight, experts)
        in_grads.append(returned(partial_rows))
        weight = None
        for chunk, share in enumerate(shares):
            left = shifted(share, "node", 2)
            right = shifted(share, "node", -2)
            other = jnp.where(even, right, left)
            near = swapped((share.astype(F32) + other.astype(F32)).astype(BF16), "node", 1)
            weight = combine_call(chunk, stepped, left, right, near, weight)
    return (weight[None, None], moment[None, None], jnp.stack(in_grads))


def solution(mesh):
    return jax.shard_map(
        on_device,
        mesh=mesh,
        in_specs=(
            P(None, ("expert", "node"), None),
            P(None, ("expert", "node")),
            P(None, ("expert", "node"), None),
            P("node", "expert", None, None),
            P("node", "expert", None, None),
        ),
        out_specs=(
            P("node", "expert", None, None),
            P("node", "expert", None, None),
            P(None, ("expert", "node"), None),
        ),
        check_vma=False,
    )
```

```python
import math

import jax
import jax.numpy as jnp
from jax import lax
from jax.experimental import pallas as pl
from jax.experimental.pallas import tpu as pltpu
from jax.sharding import PartitionSpec as P


ROUNDS = 2
NS_STEPS = 3
LEAD, LINEAR, QUADRATIC = 3.4445, -4.775, 2.0315
F32 = jnp.float32
BF16 = jnp.bfloat16
VMEM = pl.BlockSpec(memory_space=pltpu.VMEM)
SMEM = pl.BlockSpec(memory_space=pltpu.SMEM)
ANY = pl.BlockSpec(memory_space=pl.ANY)


def limit(mebibytes):
    return pltpu.CompilerParams(vmem_limit_bytes=mebibytes << 20)


def swapped(block, axis, bit):
    return lax.ppermute(block, axis, [(i, i ^ bit) for i in range(lax.axis_size(axis))])


def crossed(block, axis, way):
    count = lax.axis_size(axis)
    return lax.ppermute(
        block, axis, [((i + (-way if i % 2 else way)) % count, i) for i in range(count)]
    )


def dot(a, b):
    return jnp.dot(a, b, preferred_element_type=F32)


def dot_first(a, b):
    return lax.dot_general(a, b, (((0,), (0,)), ((), ())), preferred_element_type=F32)


def dot_last(a, b):
    return lax.dot_general(a, b, (((1,), (1,)), ((), ())), preferred_element_type=F32)


def factors(gram):
    rest, lead = None, 1.0
    for sweep in range(NS_STEPS):
        wide = gram.astype(F32)
        polynom_wide = LINEAR * wide + QUADRATIC * dot(gram, gram)
        polynom = polynom_wide.astype(BF16)
        if sweep == 0:
            rest = polynom_wide
        else:
            rest = lead * polynom_wide + LEAD * rest + dot(rest.astype(BF16), polynom)
        lead = lead * LEAD
        if sweep < NS_STEPS - 1:
            half = (LEAD * wide + dot(gram, polynom)).astype(BF16)
            gram = (LEAD * half.astype(F32) + dot(half, polynom)).astype(BF16)
    return rest, lead


def mixed(stepped, first, second, near):
    total = first[...].astype(F32) + second[...].astype(F32) + near[...].astype(F32)
    return 0.4 * stepped[...] + 0.15 * total


def split(depth):
    half = depth // 2
    return half, (half, 3 * half // 4, half // 4)


def ahead_kernel(blocks, refs):
    names = iter(refs)
    rows = [next(names) for _ in range(blocks)]
    weight, pre = next(names), next(names)
    shaped = weight[...].astype(BF16)
    count, depth = rows[0].shape[0], weight.shape[0]
    for block in range(blocks):
        pre[pl.ds(block * count, count), :] = dot(rows[block][:, :depth], shaped)


def ahead_call(rows, weight):
    width = weight.shape[1]
    total = len(rows) * rows[0].shape[0]
    return pl.pallas_call(
        lambda *refs: ahead_kernel(len(rows), refs),
        out_shape=jax.ShapeDtypeStruct((total, width), F32),
        in_specs=[VMEM] * (len(rows) + 1),
        out_specs=VMEM,
        compiler_params=limit(16),
        name="ahead",
    )(*rows, weight)


def ahead_mixed_kernel(blocks, refs):
    names = iter(refs)
    rows = [next(names) for _ in range(blocks)]
    parts = [next(names) for _ in range(4)]
    weight, pre = next(names), next(names)
    value = mixed(*parts)
    weight[...] = value
    shaped = value.astype(BF16)
    count, depth = rows[0].shape[0], value.shape[0]
    for block in range(blocks):
        pre[pl.ds(block * count, count), :] = dot(rows[block][:, :depth], shaped)


def ahead_mixed_call(rows, parts):
    half, width = parts[0].shape
    total = len(rows) * rows[0].shape[0]
    return pl.pallas_call(
        lambda *refs: ahead_mixed_kernel(len(rows), refs),
        out_shape=[
            jax.ShapeDtypeStruct((half, width), F32),
            jax.ShapeDtypeStruct((total, width), F32),
        ],
        in_specs=[VMEM] * (len(rows) + 4),
        out_specs=[VMEM] * 2,
        compiler_params=limit(16),
        name="ahead_mixed",
    )(*rows, *parts)


def round_kernel(blocks, place, fresh, refs):
    names = iter(refs)
    rows_refs = [next(names) for _ in range(blocks)]
    grad_refs = [next(names) for _ in range(blocks)]
    route, mine, pre_ref, moment_ref = (next(names) for _ in range(4))
    weight_refs = [next(names) for _ in range(1 if fresh else 5)]
    moment_out, slopes_out, weight_out = (next(names) for _ in range(3))
    stepped_out = [next(names) for _ in range(2)]
    share_out = [next(names) for _ in range(2)]
    piece_out = [next(names) for _ in range(2)]
    rows, grads, pre, weight, moment, slopes, shares, moment_low, sems = names
    depth, width = weight.shape
    count = rows_refs[0].shape[0]
    half, pieces = split(depth)
    factor = 1.0 / math.sqrt(depth)
    step_size = 0.1 * math.sqrt(depth)
    used = iter(range(64))
    pending = []

    def copy(source, target):
        made = pltpu.make_async_copy(source, target, sems.at[next(used)])
        made.start()
        return made

    arrivals = []
    for block in range(blocks):
        span = pl.ds(block * count, count)
        arrivals.append(
            (
                copy(pre_ref.at[span, :], pre.at[span, :]),
                copy(grad_refs[block].at[:, pl.ds(place, width)], grads.at[span, :]),
                copy(rows_refs[block].at[:, pl.ds(0, depth)], rows.at[span, :]),
            )
        )
    moment_in = copy(moment_ref, moment)
    upper, lower = pl.ds(0, half), pl.ds(half, half)
    if fresh:
        weight_in = copy(weight_refs[0], weight)
    else:
        weight_in = copy(weight_refs[0], weight.at[upper, :])
        value = mixed(*weight_refs[1:])
        weight[lower, :] = value
        shaped = value.astype(BF16)
    columns = route[...].T
    lanes = route.shape[1]
    for block in range(blocks):
        for item in arrivals[block]:
            item.wait()
        span = pl.ds(block * count, count)
        value = pre[span, :]
        if not fresh:
            value = value + dot(rows[span, half:], shaped)
        value = value * factor
        for piece in range(count // lanes):
            index = block * (count // lanes) + piece
            keep = columns[:, index : index + 1] == mine[0]
            piece_span = pl.ds(index * lanes, lanes)
            slope = grads[piece_span, :].astype(F32) * 2.0
            slope = slope * jnp.maximum(value[piece * lanes : (piece + 1) * lanes, :], 0.0)
            slopes[piece_span, :] = jnp.where(keep, slope, 0.0).astype(BF16)
    pending.append(copy(slopes, slopes_out))
    moment_in.wait()
    tile = min(256, depth)

    def accumulate(i, total):
        span = pl.ds(pl.multiple_of(i * tile, tile), tile)
        value = 0.9 * moment[span, :] + dot_first(rows[:, span], slopes[...]) * factor
        moment[span, :] = value
        moment_low[span, :] = value.astype(BF16)
        return total + jnp.sum(value * value, axis=0, keepdims=True)

    total = lax.fori_loop(0, depth // tile, accumulate, jnp.zeros((1, width), F32))
    pending.append(copy(moment, moment_out))
    weight_in.wait()
    kept = copy(weight, weight_out)
    scale = 1.0 / (jnp.sqrt(jnp.sum(total)) + 1e-07)
    gram = (dot_first(moment_low[...], moment_low[...]) * (scale * scale)).astype(BF16)
    rest, lead = factors(gram)
    rest = rest.astype(BF16)
    kept.wait()
    for index, span in enumerate((upper, lower)):
        low = moment_low[span, :]
        orthog = scale * (lead * low.astype(F32) + dot(low, rest))
        value = weight[span, :] - step_size * orthog
        weight[span, :] = value
        shares[span, :] = value.astype(BF16)
        pending.append(copy(shares.at[span, :], share_out[index]))
        if index:
            first = pl.ds(half, pieces[1])
            second = pl.ds(half + pieces[1], pieces[2])
            pending.append(copy(shares.at[first, :], piece_out[0]))
            pending.append(copy(shares.at[second, :], piece_out[1]))
        pending.append(copy(weight.at[span, :], stepped_out[index]))
    for item in pending:
        item.wait()


def round_call(rows, grads, place, route, mine, pre, weight, moment):
    depth, width = moment.shape
    blocks = len(rows)
    total = blocks * rows[0].shape[0]
    half, pieces = split(depth)
    fresh = len(weight) == 1
    shape = jax.ShapeDtypeStruct
    result = pl.pallas_call(
        lambda *refs: round_kernel(blocks, place, fresh, refs),
        out_shape=[
            shape((depth, width), F32),
            shape((total, width), BF16),
            shape((depth, width), F32),
            shape((half, width), F32),
            shape((half, width), F32),
            shape((half, width), BF16),
            shape((half, width), BF16),
            shape((pieces[1], width), BF16),
            shape((pieces[2], width), BF16),
        ],
        in_specs=[ANY] * (2 * blocks) + [VMEM, SMEM, ANY, ANY, ANY] + [VMEM] * (len(weight) - 1),
        out_specs=[ANY] * 9,
        scratch_shapes=[
            pltpu.VMEM((total, depth), BF16),
            pltpu.VMEM((total, width), BF16),
            pltpu.VMEM((total, width), F32),
            pltpu.VMEM((depth, width), F32),
            pltpu.VMEM((depth, width), F32),
            pltpu.VMEM((total, width), BF16),
            pltpu.VMEM((depth, width), BF16),
            pltpu.VMEM((depth, width), BF16),
            pltpu.SemaphoreType.DMA((64,)),
        ],
        compiler_params=limit(24),
        name="muon_round",
    )(*rows, *grads, route, mine, pre, moment, *weight)
    return result[0], result[1], result[2], result[3:5], result[5:7], result[7:]


def backward_kernel(slopes, weight, keep, send):
    depth = weight.shape[0]
    factor = 1.0 / math.sqrt(depth)
    shaped = weight[...].astype(BF16)
    half, count = keep.shape[:2]
    for block in range(2 * half):
        part = slopes[pl.ds(block * count, count), :]
        out = keep if block < half else send
        out[block % half] = (dot_last(part, shaped) * factor).astype(BF16)


def backward_call(slopes, weight, blocks):
    depth = weight.shape[0]
    shape = jax.ShapeDtypeStruct((blocks // 2, slopes.shape[0] // blocks, depth), BF16)
    return pl.pallas_call(
        backward_kernel,
        out_shape=[shape, shape],
        in_specs=[VMEM, VMEM],
        out_specs=[VMEM, VMEM],
        compiler_params=limit(16),
        name="row_gradients",
    )(slopes, weight)


def place_call(function, index, count, parts, buffer):
    block = parts[0].shape
    rest = (0,) * (len(block) - 1)
    extra = [] if buffer is None else [buffer]

    def kernel(*refs):
        refs[-1][...] = function(*refs[: len(parts)])

    return pl.pallas_call(
        kernel,
        grid=(1,),
        out_shape=jax.ShapeDtypeStruct((count * block[0],) + block[1:], parts[0].dtype),
        in_specs=[pl.BlockSpec(block, lambda i: (0,) + rest)] * len(parts) + [ANY] * len(extra),
        out_specs=pl.BlockSpec(block, lambda i: (index,) + rest),
        input_output_aliases={len(parts): 0} if extra else {},
        compiler_params=limit(12),
    )(*parts, *extra)


def on_device(tokens, routing, out_grad, weights, momentum):
    experts = lax.axis_size("expert")
    bits = []
    bit = experts // 2
    while bit:
        bits.append(bit)
        bit //= 2
    weight = weights[0, 0]
    moment = momentum[0, 0]
    depth = weight.shape[0]
    half, pieces = split(depth)
    mine = lax.axis_index("expert").astype(jnp.int32).reshape(1)

    def gathered(own):
        held = [own]
        for bit in bits:
            held = held + [swapped(item, "expert", bit) for item in held]
        return held

    in_grad = None
    rows = [gathered(tokens[0])]
    grads = [gathered(out_grad[0])]
    routes = gathered(routing)
    packed = jnp.concatenate([tokens[1], out_grad[1]], axis=1)
    rows.append(gathered(packed))
    grads.append(rows[1])
    pre = ahead_call(rows[0], weight)
    weight_parts = [weight]
    for index in range(ROUNDS):
        route = jnp.concatenate([item[index] for item in routes]).reshape(-1, 128)
        moment, slopes, weight, stepped, shares, extra = round_call(
            rows[index], grads[index], depth if index else 0, route, mine, pre,
            weight_parts, moment,
        )
        firsts = []
        for share in (shares[0], *extra):
            firsts.append(crossed(share, "node", 2))
        seconds = []
        for share in shares:
            seconds.append(crossed(share, "node", -2))
        firsts = [firsts[0], jnp.concatenate(firsts[1:])]
        nears = []
        for piece, share in enumerate(shares):
            pair = (share.astype(F32) + firsts[piece].astype(F32)).astype(BF16)
            nears.append(swapped(pair, "node", 1))
        keep, send = backward_call(slopes, weight, experts)
        for bit in reversed(bits):
            back = swapped(send, "expert", bit)
            if keep.shape[0] > 1:
                keep, send = jnp.split(keep + back, 2)
        in_grad = place_call(lambda a, b: a[...] + b[...], index, ROUNDS, [keep, back], in_grad)
        halves = [
            [stepped[piece], firsts[piece], seconds[piece], nears[piece]]
            for piece in range(2)
        ]
        if index < ROUNDS - 1:
            upper, pre = ahead_mixed_call(rows[index + 1], halves[0])
            weight_parts = [upper, *halves[1]]
        else:
            weight = place_call(mixed, 0, 2, halves[0], None)
            weight = place_call(mixed, 1, 2, halves[1], weight)
    return (weight[None, None], moment[None, None], in_grad)


def solution(mesh):
    return jax.shard_map(
        on_device,
        mesh=mesh,
        in_specs=(
            P(None, ("expert", "node"), None),
            P(None, ("expert", "node")),
            P(None, ("expert", "node"), None),
            P("node", "expert", None, None),
            P("node", "expert", None, None),
        ),
        out_specs=(
            P("node", "expert", None, None),
            P("node", "expert", None, None),
            P(None, ("expert", "node"), None),
        ),
        check_vma=False,
    )
```

```python
import math

import jax
import jax.numpy as jnp
from jax import lax
from jax.experimental import pallas as pl
from jax.experimental.pallas import tpu as pltpu
from jax.sharding import PartitionSpec as P


ROUNDS = 2
NS_STEPS = 3
LEAD, LINEAR, QUADRATIC = 3.4445, -4.775, 2.0315
F32 = jnp.float32
BF16 = jnp.bfloat16
VMEM = pl.BlockSpec(memory_space=pltpu.VMEM)
SMEM = pl.BlockSpec(memory_space=pltpu.SMEM)
ANY = pl.BlockSpec(memory_space=pl.ANY)


def limit(mebibytes):
    return pltpu.CompilerParams(vmem_limit_bytes=mebibytes << 20)


def swapped(block, axis, bit):
    return lax.ppermute(block, axis, [(i, i ^ bit) for i in range(lax.axis_size(axis))])


def crossed(block, axis, way):
    count = lax.axis_size(axis)
    return lax.ppermute(
        block, axis, [((i + (-way if i % 2 else way)) % count, i) for i in range(count)]
    )


def dot(a, b):
    return jnp.dot(a, b, preferred_element_type=F32)


def dot_first(a, b):
    return lax.dot_general(a, b, (((0,), (0,)), ((), ())), preferred_element_type=F32)


def dot_last(a, b):
    return lax.dot_general(a, b, (((1,), (1,)), ((), ())), preferred_element_type=F32)


def factors(gram):
    rest, lead = None, 1.0
    for sweep in range(NS_STEPS):
        wide = gram.astype(F32)
        polynom_wide = LINEAR * wide + QUADRATIC * dot(gram, gram)
        polynom = polynom_wide.astype(BF16)
        if sweep == 0:
            rest = polynom_wide
        else:
            rest = lead * polynom_wide + LEAD * rest + dot(rest.astype(BF16), polynom)
        lead = lead * LEAD
        if sweep < NS_STEPS - 1:
            half = (LEAD * wide + dot(gram, polynom)).astype(BF16)
            gram = (LEAD * half.astype(F32) + dot(half, polynom)).astype(BF16)
    return rest, lead


def take(refs, start, stop):
    parts, offset = [], 0
    for ref in refs:
        low, high = max(start, offset), min(stop, offset + ref.shape[0])
        if low < high:
            parts.append(ref[low - offset : high - offset, :])
        offset += ref.shape[0]
    return parts[0] if len(parts) == 1 else jnp.concatenate(parts, axis=0)


def put(refs, start, value):
    offset, stop = 0, start + value.shape[0]
    for ref in refs:
        low, high = max(start, offset), min(stop, offset + ref.shape[0])
        if low < high:
            ref[low - offset : high - offset, :] = value[low - start : high - start, :]
        offset += ref.shape[0]


def mixed(parts, start, stop):
    stepped, first, second, near = (take(refs, start, stop) for refs in parts)
    total = first.astype(F32) + second.astype(F32) + near.astype(F32)
    return 0.4 * stepped + 0.15 * total


def split(depth):
    half, unit = depth // 2, depth // 16
    return (half, half - unit, unit), (12 * unit, 4 * unit), (half, half)


def sizes_of(arrays):
    return [len(item) for item in arrays]


def grouped(names, sizes):
    return [[next(names) for _ in range(size)] for size in sizes]


def ahead_kernel(sizes, refs):
    names = iter(refs)
    rows, parts = grouped(names, sizes[:1])[0], grouped(names, sizes[1:])
    if len(parts) == 1:
        value = parts[0][0][...]
    else:
        weight = next(names)
        value = mixed(parts, 0, weight.shape[0])
        weight[...] = value
    pre = next(names)
    shaped = value.astype(BF16)
    count, depth = rows[0].shape[0], value.shape[0]
    for block, ref in enumerate(rows):
        pre[block * count : (block + 1) * count, :] = dot(ref[:, :depth], shaped)


def ahead_call(rows, parts):
    early, width = parts[0][0].shape
    total = len(rows) * rows[0].shape[0]
    flat = [item for part in parts for item in part]
    shapes = [jax.ShapeDtypeStruct((total, width), F32)]
    if len(parts) > 1:
        shapes.insert(0, jax.ShapeDtypeStruct((early, width), F32))
    sizes = sizes_of([rows] + parts)
    return pl.pallas_call(
        lambda *refs: ahead_kernel(sizes, refs),
        out_shape=shapes,
        in_specs=[VMEM] * (len(rows) + len(flat)),
        out_specs=[VMEM] * len(shapes),
        compiler_params=limit(16),
        name="ahead",
    )(*rows, *flat)


def round_kernel(sizes, place, refs):
    names = iter(refs)
    route, mine, pre, moment = (next(names) for _ in range(4))
    rows, grads, weights, *parts = grouped(names, sizes)
    moment_out, slopes = next(names), next(names)
    depth, width = moment.shape
    _, two, _ = split(depth)
    stepped_out, share_out, one_out, two_out = grouped(names, (2, 2, 2, 2))
    late = next(names) if parts else None
    moment_low = next(names)
    count = rows[0].shape[0]
    factor = 1.0 / math.sqrt(depth)
    step_size = 0.1 * math.sqrt(depth)
    early = two[0]
    if parts:
        value = mixed(parts, early, depth)
        late[...] = value
        shaped = value.astype(BF16)
        weights = [*weights, late]
    columns = route[...].T
    lanes = route.shape[1]
    for block, ref in enumerate(rows):
        span = slice(block * count, (block + 1) * count)
        value = pre[span, :]
        if parts:
            value = value + dot(ref[:, early:depth], shaped)
        value = value * factor
        for piece in range(count // lanes):
            index = block * (count // lanes) + piece
            keep = columns[:, index : index + 1] == mine[0]
            part = slice(piece * lanes, (piece + 1) * lanes)
            slope = grads[block][part, place : place + width].astype(F32) * 2.0
            slope = slope * jnp.maximum(value[part, :], 0.0)
            slope = jnp.where(keep, slope, 0.0).astype(BF16)
            slopes[index * lanes : (index + 1) * lanes, :] = slope
    tile = min(256, depth)
    total = jnp.zeros((1, width), F32)
    for start in range(0, depth, tile):
        span = slice(start, start + tile)
        value = None
        for block, ref in enumerate(rows):
            term = dot_first(ref[:, span], slopes[block * count : (block + 1) * count, :])
            value = term if value is None else value + term
        value = 0.9 * moment[span, :] + value * factor
        moment_out[span, :] = value
        moment_low[span, :] = value.astype(BF16)
        total = total + jnp.sum(value * value, axis=0, keepdims=True)
    scale = 1.0 / (jnp.sqrt(jnp.sum(total)) + 1e-07)
    gram = (dot_first(moment_low[...], moment_low[...]) * (scale * scale)).astype(BF16)
    rest, lead = factors(gram)
    rest = rest.astype(BF16)
    for start in range(0, depth, tile):
        low = moment_low[start : start + tile, :]
        orthog = scale * (lead * low.astype(F32) + dot(low, rest))
        value = take(weights, start, start + tile) - step_size * orthog
        put(stepped_out, start, value)
        share = value.astype(BF16)
        put(share_out, start, share)
        put([share_out[0], *one_out], start, share)
        put(two_out, start, share)


def round_call(rows, grads, place, route, mine, pre, weight, moment, parts):
    depth, width = moment.shape
    total = len(rows) * rows[0].shape[0]
    one, two, near = split(depth)

    def shapes(counts, kind):
        return [jax.ShapeDtypeStruct((count, width), kind) for count in counts]

    flat = [item for part in parts for item in part]
    sizes = sizes_of([rows, grads, [weight]] + parts)
    out = shapes((depth,), F32) + shapes((total,), BF16) + shapes(two, F32)
    out = out + shapes(near + one[1:] + two, BF16) + shapes(two[1:] if parts else (), F32)
    result = pl.pallas_call(
        lambda *refs: round_kernel(sizes, place, refs),
        out_shape=out,
        in_specs=[VMEM, SMEM] + [VMEM] * (3 + 2 * len(rows) + len(flat)),
        out_specs=[VMEM] * len(out),
        scratch_shapes=[pltpu.VMEM((depth, width), BF16)],
        compiler_params=limit(24),
        name="muon_round",
    )(route, mine, pre, moment, *rows, *grads, weight, *flat)
    shares = result[4:6]
    return (
        result[0], result[1], result[2:4], shares, [shares[0], *result[6:8]], result[8:10],
        [weight, *result[10:]],
    )


def backward_kernel(refs):
    slopes, *weights, keep, send = refs
    depth = keep.shape[2]
    factor = 1.0 / math.sqrt(depth)
    shaped = take(weights, 0, depth).astype(BF16)
    half, count = keep.shape[:2]
    for block in range(2 * half):
        part = slopes[block * count : (block + 1) * count, :]
        out = keep if block < half else send
        out[block % half] = (dot_last(part, shaped) * factor).astype(BF16)


def backward_call(slopes, weights, blocks):
    depth = sum(item.shape[0] for item in weights)
    shape = jax.ShapeDtypeStruct((blocks // 2, slopes.shape[0] // blocks, depth), BF16)
    return pl.pallas_call(
        lambda *refs: backward_kernel(refs),
        out_shape=[shape, shape],
        in_specs=[VMEM] * (1 + len(weights)),
        out_specs=[VMEM, VMEM],
        compiler_params=limit(16),
        name="row_gradients",
    )(slopes, *weights)


def average_call(parts, start, stop, depth, buffer):
    flat = [item for part in parts for item in part]
    sizes = sizes_of(parts)
    extra = [] if buffer is None else [buffer]
    width = flat[0].shape[1]

    def kernel(*refs):
        names = iter(refs)
        groups = grouped(names, sizes)
        out, value, sem = list(names)[len(extra) :]
        value[...] = mixed(groups, start, stop)
        made = pltpu.make_async_copy(value, out.at[pl.ds(start, stop - start), :], sem)
        made.start()
        made.wait()

    return pl.pallas_call(
        kernel,
        out_shape=jax.ShapeDtypeStruct((depth, width), F32),
        in_specs=[VMEM] * len(flat) + [ANY] * len(extra),
        out_specs=ANY,
        scratch_shapes=[pltpu.VMEM((stop - start, width), F32), pltpu.SemaphoreType.DMA(())],
        input_output_aliases={len(flat): 0} if extra else {},
        compiler_params=limit(12),
        name="average",
    )(*flat, *extra)


def place_call(function, index, count, parts, buffer):
    block = parts[0].shape
    rest = (0,) * (len(block) - 1)
    extra = [] if buffer is None else [buffer]

    def kernel(*refs):
        refs[-1][...] = function(*refs[: len(parts)])

    return pl.pallas_call(
        kernel,
        grid=(1,),
        out_shape=jax.ShapeDtypeStruct((count * block[0],) + block[1:], parts[0].dtype),
        in_specs=[pl.BlockSpec(block, lambda i: (0,) + rest)] * len(parts) + [ANY] * len(extra),
        out_specs=pl.BlockSpec(block, lambda i: (index,) + rest),
        input_output_aliases={len(parts): 0} if extra else {},
        compiler_params=limit(12),
    )(*parts, *extra)


def on_device(tokens, routing, out_grad, weights, momentum):
    experts = lax.axis_size("expert")
    bits = []
    bit = experts // 2
    while bit:
        bits.append(bit)
        bit //= 2
    weight = weights[0, 0]
    moment = momentum[0, 0]
    depth = weight.shape[0]
    _, two, _ = split(depth)
    mine = lax.axis_index("expert").astype(jnp.int32).reshape(1)

    def gathered(own):
        held = [own]
        for bit in bits:
            held = held + [swapped(item, "expert", bit) for item in held]
        return held

    in_grad = None
    waiting = []
    first_rows = tokens[0]
    rest_tokens, rest_grad, first_rows = lax.optimization_barrier((tokens, out_grad, first_rows))
    rows = [gathered(first_rows)]
    routes = gathered(routing)
    grads = [gathered(rest_grad[0])]
    packed = jnp.concatenate([rest_tokens[1], rest_grad[1]], axis=1)
    rows.append(gathered(packed))
    grads.append(rows[1])
    (pre,) = ahead_call(rows[0], [[weight]])
    parts = []
    for index in range(ROUNDS):
        route = jnp.concatenate([item[index] for item in routes]).reshape(-1, 128)
        moment, slopes, stepped, shares, ones, twos, pieces = round_call(
            rows[index], grads[index], depth if index else 0, route, mine, pre,
            weight, moment, parts,
        )
        firsts = []
        for share in ones:
            firsts.append(crossed(share, "node", 2))
        seconds = []
        for share in twos:
            seconds.append(crossed(share, "node", -2))
        nears = []
        for piece, other in enumerate((firsts[0], jnp.concatenate(firsts[1:]))):
            pair = (shares[piece].astype(F32) + other.astype(F32)).astype(BF16)
            nears.append(swapped(pair, "node", 1))
        keep, send = backward_call(slopes, pieces, experts)
        for bit in reversed(bits):
            back = swapped(send, "expert", bit)
            if keep.shape[0] > 1:
                keep, send = jnp.split(keep + back, 2)
        waiting.append([keep, back])
        parts = [list(stepped), firsts, seconds, nears]
        if index < ROUNDS - 1:
            weight, pre = ahead_call(rows[index + 1], [stepped[:1], firsts[:2], seconds[:1], nears])
        else:
            for done, pair in enumerate(waiting):
                in_grad = place_call(lambda a, b: a[...] + b[...], done, ROUNDS, pair, in_grad)
            weight = average_call(
                [stepped[:1], firsts[:2], seconds[:1], nears], 0, two[0], depth, None
            )
            weight = average_call(parts, two[0], depth, depth, weight)
    return (weight[None, None], moment[None, None], in_grad)


def solution(mesh):
    return jax.shard_map(
        on_device,
        mesh=mesh,
        in_specs=(
            P(None, ("expert", "node"), None),
            P(None, ("expert", "node")),
            P(None, ("expert", "node"), None),
            P("node", "expert", None, None),
            P("node", "expert", None, None),
        ),
        out_specs=(
            P("node", "expert", None, None),
            P("node", "expert", None, None),
            P(None, ("expert", "node"), None),
        ),
        check_vma=False,
    )
```

```python
import math

import jax
import jax.numpy as jnp
from jax import lax
from jax.experimental import pallas as pl
from jax.experimental.pallas import tpu as pltpu
from jax.sharding import PartitionSpec as P


ROUNDS = 2
NS_STEPS = 3
LEAD, LINEAR, QUADRATIC = 3.4445, -4.775, 2.0315
F32 = jnp.float32
BF16 = jnp.bfloat16
VMEM = pl.BlockSpec(memory_space=pltpu.VMEM)
SMEM = pl.BlockSpec(memory_space=pltpu.SMEM)
ANY = pl.BlockSpec(memory_space=pl.ANY)


def limit(mebibytes):
    return pltpu.CompilerParams(vmem_limit_bytes=mebibytes << 20)


def swapped(block, axis, bit):
    return lax.ppermute(block, axis, [(i, i ^ bit) for i in range(lax.axis_size(axis))])


def crossed(block, axis, way):
    count = lax.axis_size(axis)
    return lax.ppermute(
        block, axis, [((i + (-way if i % 2 else way)) % count, i) for i in range(count)]
    )


def dot(a, b):
    return jnp.dot(a, b, preferred_element_type=F32)


def dot_first(a, b):
    return lax.dot_general(a, b, (((0,), (0,)), ((), ())), preferred_element_type=F32)


def dot_last(a, b):
    return lax.dot_general(a, b, (((1,), (1,)), ((), ())), preferred_element_type=F32)


def factors(gram):
    rest, lead = None, 1.0
    for sweep in range(NS_STEPS):
        wide = gram.astype(F32)
        polynom_wide = LINEAR * wide + QUADRATIC * dot(gram, gram)
        polynom = polynom_wide.astype(BF16)
        if sweep == 0:
            rest = polynom_wide
        else:
            rest = lead * polynom_wide + LEAD * rest + dot(rest.astype(BF16), polynom)
        lead = lead * LEAD
        if sweep < NS_STEPS - 1:
            half = (LEAD * wide + dot(gram, polynom)).astype(BF16)
            gram = (LEAD * half.astype(F32) + dot(half, polynom)).astype(BF16)
    return rest, lead


def take(refs, start, stop):
    parts, offset = [], 0
    for ref in refs:
        low, high = max(start, offset), min(stop, offset + ref.shape[0])
        if low < high:
            parts.append(ref[low - offset : high - offset, :])
        offset += ref.shape[0]
    return parts[0] if len(parts) == 1 else jnp.concatenate(parts, axis=0)


def put(refs, start, value):
    offset, stop = 0, start + value.shape[0]
    for ref in refs:
        low, high = max(start, offset), min(stop, offset + ref.shape[0])
        if low < high:
            ref[low - offset : high - offset, :] = value[low - start : high - start, :]
        offset += ref.shape[0]


def mixed(parts, start, stop):
    stepped, first, second, near = (take(refs, start, stop) for refs in parts)
    total = first.astype(F32) + second.astype(F32) + near.astype(F32)
    return 0.4 * stepped + 0.15 * total


def split(depth):
    half, unit = depth // 2, depth // 16
    return (half, half - unit, unit), (12 * unit, 4 * unit), (half, half)


def sizes_of(arrays):
    return [len(item) for item in arrays]


def grouped(names, sizes):
    return [[next(names) for _ in range(size)] for size in sizes]


def ahead_kernel(sizes, refs):
    names = iter(refs)
    rows, parts = grouped(names, sizes[:1])[0], grouped(names, sizes[1:])
    if len(parts) == 1:
        value = parts[0][0][...]
    else:
        weight = next(names)
        value = mixed(parts, 0, weight.shape[0])
        weight[...] = value
    pre = next(names)
    shaped = value.astype(BF16)
    count, depth = rows[0].shape[0], value.shape[0]
    for block, ref in enumerate(rows):
        pre[block * count : (block + 1) * count, :] = dot(ref[:, :depth], shaped)


def ahead_call(rows, parts, early):
    width = parts[0][0].shape[1]
    total = len(rows) * rows[0].shape[0]
    flat = [item for part in parts for item in part]
    shapes = [jax.ShapeDtypeStruct((total, width), F32)]
    if len(parts) > 1:
        shapes.insert(0, jax.ShapeDtypeStruct((early, width), F32))
    sizes = sizes_of([rows] + parts)
    return pl.pallas_call(
        lambda *refs: ahead_kernel(sizes, refs),
        out_shape=shapes,
        in_specs=[VMEM] * (len(rows) + len(flat)),
        out_specs=[VMEM] * len(shapes),
        compiler_params=limit(16),
        name="ahead",
    )(*rows, *flat)


def slope_rows(route, mine, rows, grads, place, pre_of, slopes):
    columns = route[...].T
    lanes = route.shape[1]
    width = slopes.shape[1]
    for block, ref in enumerate(rows):
        count = ref.shape[0]
        value = pre_of(block, ref)
        for piece in range(count // lanes):
            index = block * (count // lanes) + piece
            keep = columns[:, index : index + 1] == mine[0]
            part = slice(piece * lanes, (piece + 1) * lanes)
            slope = grads[block][part, place : place + width].astype(F32) * 2.0
            slope = slope * jnp.maximum(value[part, :], 0.0)
            slope = jnp.where(keep, slope, 0.0).astype(BF16)
            slopes[index * lanes : (index + 1) * lanes, :] = slope


def weight_gradient(rows, slopes, span):
    value = None
    for block, ref in enumerate(rows):
        count = ref.shape[0]
        term = dot_first(ref[:, span], slopes[block * count : (block + 1) * count, :])
        value = term if value is None else value + term
    return value


def tiles(depth):
    tile = min(256, depth)
    return [slice(start, start + tile) for start in range(0, depth, tile)]


def local_kernel(sizes, refs):
    names = iter(refs)
    route, mine, weight, moment = (next(names) for _ in range(4))
    rows, grads = grouped(names, sizes)
    partial, slopes = names
    depth = weight.shape[0]
    factor = 1.0 / math.sqrt(depth)
    shaped = weight[...].astype(BF16)
    slope_rows(
        route, mine, rows, grads, 0, lambda block, ref: dot(ref[...], shaped) * factor, slopes
    )
    for span in tiles(depth):
        partial[span, :] = 0.9 * moment[span, :] + weight_gradient(rows, slopes, span) * factor


def local_call(rows, grads, route, mine, weight, moment):
    depth, width = weight.shape
    total = len(rows) * rows[0].shape[0]
    sizes = sizes_of([rows, grads])
    return pl.pallas_call(
        lambda *refs: local_kernel(sizes, refs),
        out_shape=[
            jax.ShapeDtypeStruct((depth, width), F32),
            jax.ShapeDtypeStruct((total, width), BF16),
        ],
        in_specs=[VMEM, SMEM] + [VMEM] * (2 + 2 * len(rows)),
        out_specs=[VMEM] * 2,
        compiler_params=limit(16),
        name="local_rows",
    )(route, mine, weight, moment, *rows, *grads)


def round_kernel(sizes, place, decay, refs):
    names = iter(refs)
    route, mine, pre, moment = (next(names) for _ in range(4))
    rows, grads, weights, *parts = grouped(names, sizes)
    moment_out, slopes, moment_low, rest_out, scale_out, stepped, share = (
        next(names) for _ in range(7)
    )
    depth, width = moment.shape
    half, early = split(depth)[2][0], split(depth)[1][0]
    factor = 1.0 / math.sqrt(depth)
    if parts:
        late = next(names)
        value = mixed(parts, early, depth)
        late[...] = value
        shaped = value.astype(BF16)

    def pre_of(block, ref):
        count = ref.shape[0]
        value = pre[block * count : (block + 1) * count, :]
        if parts:
            value = value + dot(ref[:, early:depth], shaped)
        return value * factor

    slope_rows(route, mine, rows, grads, place, pre_of, slopes)
    total = jnp.zeros((1, width), F32)
    for span in tiles(depth):
        value = weight_gradient(rows, slopes, span) * factor
        value = (moment[span, :] if decay == 1.0 else decay * moment[span, :]) + value
        moment_out[span, :] = value
        moment_low[span, :] = value.astype(BF16)
        total = total + jnp.sum(value * value, axis=0, keepdims=True)
    scale = 1.0 / (jnp.sqrt(jnp.sum(total)) + 1e-07)
    scale_out[0] = scale
    gram = (dot_first(moment_low[...], moment_low[...]) * (scale * scale)).astype(BF16)
    rest = factors(gram)[0].astype(BF16)
    rest_out[...] = rest
    step_rows(tiles(half), weights, moment_low, rest, scale, [stepped], [[share]], 0)


def step_rows(spans, weights, moment_low, rest, scale, stepped, shares, base):
    step_size = 0.1 * math.sqrt(moment_low.shape[0])
    for span in spans:
        low = moment_low[span, :]
        orthog = scale * (LEAD**NS_STEPS * low.astype(F32) + dot(low, rest))
        value = take(weights, span.start, span.stop) - step_size * orthog
        put(stepped, span.start - base, value)
        for refs in shares:
            put(refs, span.start - base, value.astype(BF16))


def round_call(rows, grads, place, decay, route, mine, pre, weights, moment, parts):
    depth, width = moment.shape
    total = len(rows) * rows[0].shape[0]
    half, late = split(depth)[2][0], split(depth)[1][1]
    shape = jax.ShapeDtypeStruct
    flat = [item for part in parts for item in part]
    sizes = sizes_of([rows, grads, weights] + parts)
    out = [
        shape((depth, width), F32),
        shape((total, width), BF16),
        shape((depth, width), BF16),
        shape((width, width), BF16),
        shape((1,), F32),
        shape((half, width), F32),
        shape((half, width), BF16),
    ]
    specs = [VMEM] * 4 + [SMEM] + [VMEM] * 2
    if parts:
        out.append(shape((late, width), F32))
        specs.append(VMEM)
    return pl.pallas_call(
        lambda *refs: round_kernel(sizes, place, decay, refs),
        out_shape=out,
        in_specs=[VMEM, SMEM] + [VMEM] * (2 + 2 * len(rows) + len(weights) + len(flat)),
        out_specs=specs,
        compiler_params=limit(16),
        name="muon_round",
    )(route, mine, pre, moment, *rows, *grads, *weights, *flat)


def second_kernel(count, refs):
    moment_low, rest, scale, share, *names = refs
    weights, names = names[:count], iter(names[count:])
    stepped, share_out, *rest_out = names
    ones, twos = rest_out[:2], rest_out[2:]
    depth = moment_low.shape[0]
    half = share.shape[0]
    put(twos, 0, share[...])
    spans = [span for span in tiles(depth) if span.start >= half]
    step_rows(
        spans, weights, moment_low, rest[...], scale[0], [stepped], [[share_out], ones], half
    )
    put(twos, half, share_out[...])


def second_call(moment_low, rest, scale, share, weights):
    depth, width = moment_low.shape
    one, two, near = split(depth)
    shape = jax.ShapeDtypeStruct
    out = [shape((near[1], width), F32)]
    out = out + [shape((size, width), BF16) for size in near[1:] + one[1:] + two]
    result = pl.pallas_call(
        lambda *refs: second_kernel(len(weights), refs),
        out_shape=out,
        in_specs=[VMEM] * 2 + [SMEM] + [VMEM] * (1 + len(weights)),
        out_specs=[VMEM] * len(out),
        compiler_params=limit(12),
        name="second_half",
    )(moment_low, rest, scale, share, *weights)
    return result[0], result[1], [share, *result[2:4]], result[4:]


def backward_kernel(sizes, refs):
    names = iter(refs)
    slopes, weights = grouped(names, sizes)
    keep, send = names
    depth = keep.shape[2]
    factor = 1.0 / math.sqrt(depth)
    shaped = take(weights, 0, depth).astype(BF16)
    half, count = keep.shape[:2]
    for block in range(2 * half):
        place = block // len(slopes) * count
        part = slopes[block % len(slopes)][place : place + count, :]
        out = keep if block < half else send
        out[block % half] = (dot_last(part, shaped) * factor).astype(BF16)


def backward_call(slopes, weights, blocks):
    depth = sum(item.shape[0] for item in weights)
    count = sum(item.shape[0] for item in slopes) // blocks
    shape = jax.ShapeDtypeStruct((blocks // 2, count, depth), BF16)
    sizes = sizes_of([slopes, weights])
    return pl.pallas_call(
        lambda *refs: backward_kernel(sizes, refs),
        out_shape=[shape, shape],
        in_specs=[VMEM] * (len(slopes) + len(weights)),
        out_specs=[VMEM, VMEM],
        compiler_params=limit(16),
        name="row_gradients",
    )(*slopes, *weights)


def halve_call(keep, back):
    half = keep.shape[0] // 2
    shape = jax.ShapeDtypeStruct((half,) + keep.shape[1:], keep.dtype)

    def kernel(keep, back, first, second):
        first[...] = keep[:half] + back[:half]
        second[...] = keep[half:] + back[half:]

    return pl.pallas_call(
        kernel,
        out_shape=[shape, shape],
        in_specs=[VMEM] * 2,
        out_specs=[VMEM] * 2,
        compiler_params=limit(12),
        name="halve",
    )(keep, back)


def average_call(parts, start, stop, depth, buffer):
    flat = [item for part in parts for item in part]
    sizes = sizes_of(parts)
    extra = [] if buffer is None else [buffer]
    width = flat[0].shape[1]

    def kernel(*refs):
        names = iter(refs)
        groups = grouped(names, sizes)
        out, value, sem = list(names)[len(extra) :]
        value[...] = mixed(groups, start, stop)
        made = pltpu.make_async_copy(value, out.at[pl.ds(start, stop - start), :], sem)
        made.start()
        made.wait()

    return pl.pallas_call(
        kernel,
        out_shape=jax.ShapeDtypeStruct((depth, width), F32),
        in_specs=[VMEM] * len(flat) + [ANY] * len(extra),
        out_specs=ANY,
        scratch_shapes=[pltpu.VMEM((stop - start, width), F32), pltpu.SemaphoreType.DMA(())],
        input_output_aliases={len(flat): 0} if extra else {},
        compiler_params=limit(12),
        name="average",
    )(*flat, *extra)


def place_call(function, index, count, parts, buffer):
    block = parts[0].shape
    rest = (0,) * (len(block) - 1)
    extra = [] if buffer is None else [buffer]

    def kernel(*refs):
        refs[-1][...] = function(*refs[: len(parts)])

    return pl.pallas_call(
        kernel,
        grid=(1,),
        out_shape=jax.ShapeDtypeStruct((count * block[0],) + block[1:], parts[0].dtype),
        in_specs=[pl.BlockSpec(block, lambda i: (0,) + rest)] * len(parts) + [ANY] * len(extra),
        out_specs=pl.BlockSpec(block, lambda i: (index,) + rest),
        input_output_aliases={len(parts): 0} if extra else {},
        compiler_params=limit(12),
    )(*parts, *extra)


def on_device(tokens, routing, out_grad, weights, momentum):
    experts = lax.axis_size("expert")
    bits = []
    bit = experts // 2
    while bit:
        bits.append(bit)
        bit //= 2
    weight = weights[0, 0]
    moment = momentum[0, 0]
    depth = weight.shape[0]
    _, two, _ = split(depth)
    mine = lax.axis_index("expert").astype(jnp.int32).reshape(1)

    def gathered(own):
        held = [own]
        for bit in bits:
            moved = []
            for item in held:
                moved.append(swapped(item, "expert", bit))
            held = held + moved
        return held

    in_grad = None
    waiting = []
    own_rows, rest_tokens, rest_grad = lax.optimization_barrier(
        (tokens[0], tokens, out_grad)
    )
    own_grads = rest_grad[0]
    packed = jnp.concatenate([rest_tokens[1], rest_grad[1]], axis=1)
    first_rows = gathered(own_rows)
    routes = gathered(routing)
    first_grads = gathered(own_grads)
    later = gathered(packed)

    def route_of(index, items):
        picked = [item[index] for item in items]
        return jnp.concatenate(picked * (experts // len(picked))).reshape(-1, 128)

    moment, slopes = local_call(
        first_rows[0::2], first_grads[0::2], route_of(0, routes[0::2]), mine, weight, moment
    )
    all_slopes = [slopes]
    (pre,) = ahead_call(first_rows[1::2], [[weight]], depth)
    weights = [weight]
    parts = []
    for index in range(ROUNDS):
        if index:
            moment, slopes, low, rest, scale, stepped, share, late = round_call(
                later, later, depth, 0.9, route_of(index, routes), mine, pre, weights,
                moment, parts,
            )
            weights = [*weights, late]
            all_slopes = [slopes]
        else:
            moment, slopes, low, rest, scale, stepped, share = round_call(
                first_rows[1::2], first_grads[1::2], 0, 1.0, route_of(0, routes[1::2]),
                mine, pre, weights, moment, parts,
            )
            all_slopes.append(slopes)
        stepped_low, share_low, ones, twos = second_call(low, rest, scale, share, weights)
        firsts = []
        for item in ones:
            firsts.append(crossed(item, "node", 2))
        seconds = []
        for item in twos:
            seconds.append(crossed(item, "node", -2))
        nears = []
        others = (firsts[0], jnp.concatenate(firsts[1:]))
        for piece, item in enumerate((share, share_low)):
            pair = (item.astype(F32) + others[piece].astype(F32)).astype(BF16)
            nears.append(swapped(pair, "node", 1))
        keep, send = backward_call(all_slopes, weights, experts)
        for bit in reversed(bits):
            back = swapped(send, "expert", bit)
            if keep.shape[0] > 1:
                keep, send = halve_call(keep, back)
        waiting.append([keep, back])
        halves = [stepped, stepped_low]
        parts = [halves, firsts, seconds, nears]
        early_parts = [halves, firsts[:2], seconds[:1], nears]
        if index < ROUNDS - 1:
            upper, pre = ahead_call(later, early_parts, two[0])
            weights = [upper]
        else:
            for done, pair in enumerate(waiting):
                in_grad = place_call(lambda a, b: a[...] + b[...], done, ROUNDS, pair, in_grad)
            weight = average_call(early_parts, 0, two[0], depth, None)
            weight = average_call(parts, two[0], depth, depth, weight)
    return (weight[None, None], moment[None, None], in_grad)


def solution(mesh):
    return jax.shard_map(
        on_device,
        mesh=mesh,
        in_specs=(
            P(None, ("expert", "node"), None),
            P(None, ("expert", "node")),
            P(None, ("expert", "node"), None),
            P("node", "expert", None, None),
            P("node", "expert", None, None),
        ),
        out_specs=(
            P("node", "expert", None, None),
            P("node", "expert", None, None),
            P(None, ("expert", "node"), None),
        ),
        check_vma=False,
    )
```

```python
import math

import jax
import jax.numpy as jnp
from jax import lax
from jax.experimental import pallas as pl
from jax.experimental.pallas import tpu as pltpu
from jax.sharding import PartitionSpec as P


ROUNDS = 2
NS_STEPS = 3
LEAD, LINEAR, QUADRATIC = 3.4445, -4.775, 2.0315
F32 = jnp.float32
BF16 = jnp.bfloat16
VMEM = pl.BlockSpec(memory_space=pltpu.VMEM)
SMEM = pl.BlockSpec(memory_space=pltpu.SMEM)
ANY = pl.BlockSpec(memory_space=pl.ANY)


def limit(mebibytes):
    return pltpu.CompilerParams(vmem_limit_bytes=mebibytes << 20)


def swapped(block, axis, bit):
    return lax.ppermute(block, axis, [(i, i ^ bit) for i in range(lax.axis_size(axis))])


def crossed(block, axis, way):
    count = lax.axis_size(axis)
    return lax.ppermute(
        block, axis, [((i + (-way if i % 2 else way)) % count, i) for i in range(count)]
    )


def dot(a, b):
    return jnp.dot(a, b, preferred_element_type=F32)


def dot_first(a, b):
    return lax.dot_general(a, b, (((0,), (0,)), ((), ())), preferred_element_type=F32)


def dot_last(a, b):
    return lax.dot_general(a, b, (((1,), (1,)), ((), ())), preferred_element_type=F32)


def joined(top, corner):
    edge = top.shape[0]
    below = jnp.concatenate([top[:, edge:].T, corner], axis=1)
    return jnp.concatenate([top, below], axis=0)


def product(left, right):
    edge = left.shape[0] // 2
    return dot(left[:edge], right), dot(left[edge:], right[:, edge:])


def low(pair):
    return tuple(item.astype(BF16) for item in pair)


def mix(*terms):
    return tuple(
        sum(factor * pair[i].astype(F32) for factor, pair in terms) for i in range(2)
    )


def factors(gram):
    rest, lead = None, 1.0
    for sweep in range(NS_STEPS):
        whole = joined(*gram)
        polynom_wide = mix((LINEAR, gram), (QUADRATIC, product(whole, whole)))
        polynom = joined(*low(polynom_wide))
        if sweep == 0:
            rest = polynom_wide
        else:
            rest = mix(
                (lead, polynom_wide), (LEAD, rest), (1.0, product(joined(*low(rest)), polynom))
            )
        lead = lead * LEAD
        if sweep < NS_STEPS - 1:
            half = low(mix((LEAD, gram), (1.0, product(whole, polynom))))
            gram = low(mix((LEAD, half), (1.0, product(joined(*half), polynom))))
    return joined(*low(rest))


def take(refs, start, stop, columns=slice(None)):
    parts, offset = [], 0
    for ref in refs:
        begin, end = max(start, offset), min(stop, offset + ref.shape[0])
        if begin < end:
            parts.append(ref[begin - offset : end - offset, columns])
        offset += ref.shape[0]
    return parts[0] if len(parts) == 1 else jnp.concatenate(parts, axis=0)


def put(refs, start, value):
    offset, stop = 0, start + value.shape[0]
    for ref in refs:
        begin, end = max(start, offset), min(stop, offset + ref.shape[0])
        if begin < end:
            ref[begin - offset : end - offset, :] = value[begin - start : end - start, :]
        offset += ref.shape[0]


def mixed(parts, start, stop):
    stepped, first, second, near = (take(refs, start, stop) for refs in parts)
    total = first.astype(F32) + second.astype(F32) + near.astype(F32)
    return 0.4 * stepped + 0.15 * total


def split(depth):
    half, unit = depth // 2, depth // 16
    return (half, half - 2 * unit, 2 * unit), (12 * unit, 4 * unit)


def sizes_of(arrays):
    return [len(item) for item in arrays]


def grouped(names, sizes):
    return [[next(names) for _ in range(size)] for size in sizes]


def ahead_kernel(sizes, refs):
    names = iter(refs)
    rows, parts = grouped(names, sizes[:1])[0], grouped(names, sizes[1:])
    if len(parts) == 1:
        value = parts[0][0][...]
    else:
        weight = next(names)
        value = mixed(parts, 0, weight.shape[0])
        weight[...] = value
    pre = next(names)
    shaped = value.astype(BF16)
    place, depth = 0, value.shape[0]
    for ref in rows:
        pre[place : place + ref.shape[0], :] = dot(ref[:, :depth], shaped)
        place += ref.shape[0]


def ahead_call(rows, parts, early):
    width = parts[0][0].shape[1]
    total = sum(item.shape[0] for item in rows)
    flat = [item for part in parts for item in part]
    shapes = [jax.ShapeDtypeStruct((total, width), F32)]
    if len(parts) > 1:
        shapes.insert(0, jax.ShapeDtypeStruct((early, width), F32))
    sizes = sizes_of([rows] + parts)
    return pl.pallas_call(
        lambda *refs: ahead_kernel(sizes, refs),
        out_shape=shapes,
        in_specs=[VMEM] * (len(rows) + len(flat)),
        out_specs=[VMEM] * len(shapes),
        compiler_params=limit(16),
        name="ahead",
    )(*rows, *flat)


def slope_rows(route, mine, rows, grads, pre_of, slopes):
    columns = None if route is None else route[...].T
    place = 0
    for block, refs in enumerate(blocks_of(rows, grads)):
        count = grads[block].shape[0]
        value = pre_of(place, refs)
        lanes = count if route is None else route.shape[1]
        for start in range(0, count, lanes):
            part = slice(start, start + lanes)
            slope = grads[block][part, :].astype(F32) * 2.0 * jnp.maximum(value[part, :], 0.0)
            if route is not None:
                index = (place + start) // lanes
                slope = jnp.where(columns[:, index : index + 1] == mine[0], slope, 0.0)
            slopes[place + start : place + start + lanes, :] = slope.astype(BF16)
        place += count


def blocks_of(rows, grads):
    pieces = len(rows) // len(grads)
    return [rows[i * pieces : (i + 1) * pieces] for i in range(len(grads))]


def weight_gradient(rows, grads, slopes, span):
    value, place = None, 0
    for block, refs in enumerate(blocks_of(rows, grads)):
        count = grads[block].shape[0]
        term = dot_first(take(refs, 0, count, span), slopes[place : place + count, :])
        value = term if value is None else value + term
        place += count
    return value


def tiles(depth):
    tile = min(256, depth)
    return [slice(start, start + tile) for start in range(0, depth, tile)]


def part_kernel(sizes, decay, ready, refs):
    names = iter(refs)
    route, mine, source, moment = (next(names) for _ in range(4))
    rows, grads = grouped(names, sizes)
    partial, slopes = names
    depth = moment.shape[0]
    factor = 1.0 / math.sqrt(depth)
    shaped = None if ready else source[...].astype(BF16)

    def pre_of(place, refs):
        count = sum(ref.shape[0] for ref in refs)
        if ready:
            return source[place : place + count, :] * factor
        return dot(take(refs, 0, count), shaped) * factor

    slope_rows(route, mine, rows, grads, pre_of, slopes)
    for span in tiles(depth):
        before = moment[span, :] if decay == 1.0 else decay * moment[span, :]
        partial[span, :] = before + weight_gradient(rows, grads, slopes, span) * factor


def part_call(rows, grads, route, mine, source, moment, decay, ready):
    depth, width = moment.shape
    total = sum(item.shape[0] for item in rows)
    sizes = sizes_of([rows, grads])
    return pl.pallas_call(
        lambda *refs: part_kernel(sizes, decay, ready, refs),
        out_shape=[
            jax.ShapeDtypeStruct((depth, width), F32),
            jax.ShapeDtypeStruct((total, width), BF16),
        ],
        in_specs=[VMEM, SMEM] + [VMEM] * (2 + len(rows) + len(grads)),
        out_specs=[VMEM] * 2,
        compiler_params=limit(16),
        name="part_rows",
    )(route, mine, source, moment, *rows, *grads)


def round_kernel(sizes, decay, refs):
    names = iter(refs)
    mine, pre, moment = (next(names) for _ in range(3))
    route = None if decay < 1.0 else next(names)
    rows, grads, weights, *parts = grouped(names, sizes)
    moment_out, slopes, moment_low, rest_out, scale_out, stepped, share = (
        next(names) for _ in range(7)
    )
    depth, width = moment.shape
    half, early = split(depth)[0][0], split(depth)[1][0]
    factor = 1.0 / math.sqrt(depth)
    if parts:
        late = next(names)
        value = mixed(parts, early, depth)
        late[...] = value
        shaped = value.astype(BF16)

    def pre_of(place, refs):
        count = sum(ref.shape[0] for ref in refs)
        value = pre[place : place + count, :]
        if parts:
            value = value + dot(take(refs, 0, count, slice(early, depth)), shaped)
        return value * factor

    slope_rows(route, mine, rows, grads, pre_of, slopes)
    total = jnp.zeros((1, width), F32)
    for span in tiles(depth):
        value = weight_gradient(rows, grads, slopes, span) * factor
        value = (moment[span, :] if decay == 1.0 else decay * moment[span, :]) + value
        moment_out[span, :] = value
        moment_low[span, :] = value.astype(BF16)
        total = total + jnp.sum(value * value, axis=0, keepdims=True)
    scale = 1.0 / (jnp.sqrt(jnp.sum(total)) + 1e-07)
    scale_out[0] = scale
    edge = width // 2
    top = dot_first(moment_low[:, :edge], moment_low[...]) * (scale * scale)
    corner = dot_first(moment_low[:, edge:], moment_low[:, edge:]) * (scale * scale)
    rest = factors(low((top, corner)))
    rest_out[...] = rest
    step_rows(tiles(half), weights, moment_low, rest, scale, [stepped], [[share]], 0)


def step_rows(spans, weights, moment_low, rest, scale, stepped, shares, base):
    step_size = 0.1 * math.sqrt(moment_low.shape[0])
    for span in spans:
        low = moment_low[span, :]
        orthog = scale * (LEAD**NS_STEPS * low.astype(F32) + dot(low, rest))
        value = take(weights, span.start, span.stop) - step_size * orthog
        put(stepped, span.start - base, value)
        for refs in shares:
            put(refs, span.start - base, value.astype(BF16))


def round_call(rows, grads, decay, route, mine, pre, weights, moment, parts):
    depth, width = moment.shape
    total = sum(item.shape[0] for item in rows)
    routes = [] if decay < 1.0 else [route]
    half, late = split(depth)[0][0], split(depth)[1][1]
    shape = jax.ShapeDtypeStruct
    flat = [item for part in parts for item in part]
    sizes = sizes_of([rows, grads, weights] + parts)
    out = [
        shape((depth, width), F32),
        shape((total, width), BF16),
        shape((depth, width), BF16),
        shape((width, width), BF16),
        shape((1,), F32),
        shape((half, width), F32),
        shape((half, width), BF16),
    ]
    specs = [VMEM] * 4 + [SMEM] + [VMEM] * 2
    if parts:
        out.append(shape((late, width), F32))
        specs.append(VMEM)
    return pl.pallas_call(
        lambda *refs: round_kernel(sizes, decay, refs),
        out_shape=out,
        in_specs=[SMEM] + [VMEM] * (2 + len(routes) + sum(sizes)),
        out_specs=specs,
        compiler_params=limit(16),
        name="muon_round",
    )(mine, pre, moment, *routes, *rows, *grads, *weights, *flat)


def second_kernel(count, refs):
    moment_low, rest, scale, share, *names = refs
    weights, names = names[:count], iter(names[count:])
    stepped, *rest_out = names
    ones, twos = rest_out[:2], rest_out[2:]
    depth = moment_low.shape[0]
    half = share.shape[0]
    put(twos, 0, share[...])
    spans = [span for span in tiles(depth) if span.start >= half]
    step_rows(spans, weights, moment_low, rest[...], scale[0], [stepped], [ones], half)
    put(twos, half, take(ones, 0, depth - half))


def second_call(moment_low, rest, scale, share, weights):
    depth, width = moment_low.shape
    one, two = split(depth)
    shape = jax.ShapeDtypeStruct
    out = [shape((depth - one[0], width), F32)]
    out = out + [shape((size, width), BF16) for size in one[1:] + two]
    result = pl.pallas_call(
        lambda *refs: second_kernel(len(weights), refs),
        out_shape=out,
        in_specs=[VMEM] * 2 + [SMEM] + [VMEM] * (1 + len(weights)),
        out_specs=[VMEM] * len(out),
        compiler_params=limit(12),
        name="second_half",
    )(moment_low, rest, scale, share, *weights)
    return result[0], [share, *result[1:3]], result[3:]


def squeeze_kernel(refs):
    route, mine, *packed, rows, grads, picks = refs
    count, depth = packed[0].shape[0], rows.shape[1]
    slots = count // 2
    lanes = route.shape[1]
    kept = (route[...] == mine[0]).astype(F32)
    pieces = count // lanes
    lines = [
        jnp.concatenate([kept[i : i + 1] for i in range(b * pieces, (b + 1) * pieces)], axis=1)
        for b in range(len(packed))
    ]
    keep = jnp.concatenate(lines * (8 // len(packed)), axis=0).astype(BF16)
    before = lax.broadcasted_iota(jnp.int32, (count, count), 0)
    after = lax.broadcasted_iota(jnp.int32, (count, count), 1)
    rank = dot(keep, (before <= after).astype(BF16)) * keep.astype(F32)
    slot = (lax.broadcasted_iota(jnp.int32, (slots, count), 0) + 1).astype(F32)
    for block, ref in enumerate(packed):
        span = slice(block * slots, (block + 1) * slots)
        pick = (slot == rank[block : block + 1, :]).astype(BF16)
        picks[span, :] = pick
        rows[span, :] = dot(pick, ref[:, :depth]).astype(BF16)
        grads[span, :] = dot(pick, ref[:, depth:]).astype(BF16)


def squeeze_call(packed, route, mine, depth):
    count, total = packed[0].shape
    slots = len(packed) * (count // 2)
    shape = jax.ShapeDtypeStruct
    return pl.pallas_call(
        lambda *refs: squeeze_kernel(refs),
        out_shape=[
            shape((slots, depth), BF16),
            shape((slots, total - depth), BF16),
            shape((slots, count), BF16),
        ],
        in_specs=[VMEM, SMEM] + [VMEM] * len(packed),
        out_specs=[VMEM] * 3,
        compiler_params=limit(16),
        name="squeeze",
    )(route, mine, *packed)


def backward_kernel(sizes, where, refs):
    names = iter(refs)
    slopes, weights, picks = grouped(names, sizes)
    keep, send = names
    depth = keep.shape[2]
    factor = 1.0 / math.sqrt(depth)
    shaped = take(weights, 0, depth).astype(BF16)
    half, count = keep.shape[:2]
    step = count // 2 if picks else count
    for block in range(2 * half):
        array, place = where[block]
        part = slopes[array][place * step : (place + 1) * step, :]
        value = (dot_last(part, shaped) * factor).astype(BF16)
        if picks:
            value = dot_first(picks[0][block * step : (block + 1) * step, :], value).astype(BF16)
        out = keep if block < half else send
        out[block % half] = value


def backward_call(slopes, weights, picks, where, count):
    depth = sum(item.shape[0] for item in weights)
    shape = jax.ShapeDtypeStruct((len(where) // 2, count, depth), BF16)
    sizes = sizes_of([slopes, weights, picks])
    return pl.pallas_call(
        lambda *refs: backward_kernel(sizes, where, refs),
        out_shape=[shape, shape],
        in_specs=[VMEM] * sum(sizes),
        out_specs=[VMEM, VMEM],
        compiler_params=limit(16),
        name="backward",
    )(*slopes, *weights, *picks)


def halve_call(keep, back):
    half = keep.shape[0] // 2
    shape = jax.ShapeDtypeStruct((half,) + keep.shape[1:], keep.dtype)

    def kernel(keep, back, first, second):
        first[...] = keep[:half] + back[:half]
        second[...] = keep[half:] + back[half:]

    return pl.pallas_call(
        kernel,
        out_shape=[shape, shape],
        in_specs=[VMEM] * 2,
        out_specs=[VMEM] * 2,
        compiler_params=limit(12),
        name="halve",
    )(keep, back)


def average_call(parts, start, stop, depth, buffer):
    flat = [item for part in parts for item in part]
    sizes = sizes_of(parts)
    extra = [] if buffer is None else [buffer]
    width = flat[0].shape[1]

    def kernel(*refs):
        names = iter(refs)
        groups = grouped(names, sizes)
        out, value, sem = list(names)[len(extra) :]
        value[...] = mixed(groups, start, stop)
        made = pltpu.make_async_copy(value, out.at[pl.ds(start, stop - start), :], sem)
        made.start()
        made.wait()

    return pl.pallas_call(
        kernel,
        out_shape=jax.ShapeDtypeStruct((depth, width), F32),
        in_specs=[VMEM] * len(flat) + [ANY] * len(extra),
        out_specs=ANY,
        scratch_shapes=[pltpu.VMEM((stop - start, width), F32), pltpu.SemaphoreType.DMA(())],
        input_output_aliases={len(flat): 0} if extra else {},
        compiler_params=limit(12),
        name="average",
    )(*flat, *extra)


def place_call(function, index, count, parts, buffer):
    block = parts[0].shape
    rest = (0,) * (len(block) - 1)
    extra = [] if buffer is None else [buffer]

    def kernel(*refs):
        refs[-1][...] = function(*refs[: len(parts)])

    return pl.pallas_call(
        kernel,
        grid=(1,),
        out_shape=jax.ShapeDtypeStruct((count * block[0],) + block[1:], parts[0].dtype),
        in_specs=[pl.BlockSpec(block, lambda i: (0,) + rest)] * len(parts) + [ANY] * len(extra),
        out_specs=pl.BlockSpec(block, lambda i: (index,) + rest),
        input_output_aliases={len(parts): 0} if extra else {},
        compiler_params=limit(12),
    )(*parts, *extra)


def on_device(tokens, routing, out_grad, weights, momentum):
    experts = lax.axis_size("expert")
    bits = []
    bit = experts // 2
    while bit:
        bits.append(bit)
        bit //= 2
    weight = weights[0, 0]
    moment = momentum[0, 0]
    depth = weight.shape[0]
    _, two = split(depth)
    mine = lax.axis_index("expert").astype(jnp.int32).reshape(1)

    def gathered(own):
        held = [own]
        for bit in bits:
            moved = []
            for item in held:
                moved.append(swapped(item, "expert", bit))
            held = held + moved
        return held

    in_grad = None
    waiting = []
    count = tokens.shape[1]
    lead = count // 4
    own_rows, rest_tokens = lax.optimization_barrier((tokens[0, :lead], tokens))
    own_rest, rest_tokens, rest_grad = lax.optimization_barrier(
        (rest_tokens[0, lead:], rest_tokens, out_grad)
    )
    own_grads = rest_grad[0]
    packed = jnp.concatenate([rest_tokens[1], rest_grad[1]], axis=1)
    first_rows = list(zip(gathered(own_rows), gathered(own_rest)))

    def rows_of(blocks):
        return [piece for block in first_rows[blocks] for piece in block]

    routes = gathered(routing)
    first_grads = gathered(own_grads)
    later = gathered(packed)

    def route_of(index, items):
        picked = [item[index] for item in items]
        return jnp.concatenate(picked * (experts // len(picked))).reshape(-1, 128)

    near, direct, relayed = slice(0, None, 2), slice(1, 2), slice(3, None, 2)
    moment, slopes = part_call(
        rows_of(near), first_grads[near], route_of(0, routes[near]), mine, weight,
        moment, 0.9, False,
    )
    all_slopes = [slopes]
    (pre,) = ahead_call(rows_of(direct), [[weight]], depth)
    (relayed_pre,) = ahead_call(rows_of(relayed), [[weight]], depth)
    moment, slopes = part_call(
        rows_of(direct), first_grads[direct], route_of(0, routes[direct]), mine, pre,
        moment, 1.0, True,
    )
    all_slopes.append(slopes)
    pre = relayed_pre
    where = [[(0, block) for block in range(experts)]]
    where.insert(0, [(0, i // 2) if i % 2 == 0 else (min(i, 2), max(0, i - 3) // 2) for i in range(experts)])
    weights = [weight]
    parts, picks = [], []
    for index in range(ROUNDS):
        if index:
            moment, slopes, low, rest, scale, stepped, share, late = round_call(
                [later_rows], [later_grads], 0.9, None, mine, pre, weights, moment, parts
            )
            weights = [*weights, late]
            all_slopes = [slopes]
        else:
            moment, slopes, low, rest, scale, stepped, share = round_call(
                rows_of(relayed), first_grads[relayed], 1.0, route_of(0, routes[relayed]),
                mine, pre, weights, moment, parts,
            )
            all_slopes.append(slopes)
        stepped_low, ones, twos = second_call(low, rest, scale, share, weights)
        firsts = []
        for item in ones:
            firsts.append(crossed(item, "node", 2))
        seconds = []
        for item in twos:
            seconds.append(crossed(item, "node", -2))
        nears = []
        for piece, item in enumerate(ones):
            pair = (item.astype(F32) + firsts[piece].astype(F32)).astype(BF16)
            nears.append(swapped(pair, "node", 1))
        keep, send = backward_call(all_slopes, weights, picks, where[index], count)
        for bit in reversed(bits):
            back = swapped(send, "expert", bit)
            if keep.shape[0] > 1:
                keep, send = halve_call(keep, back)
        waiting.append([keep, back])
        halves = [stepped, stepped_low]
        parts = [halves, firsts, seconds, nears]
        early_parts = [halves, firsts[:2], seconds[:1], nears[:2]]
        if index < ROUNDS - 1:
            later_rows, later_grads, pick = squeeze_call(
                later, route_of(index + 1, routes), mine, depth
            )
            picks = [pick]
            upper, pre = ahead_call([later_rows], early_parts, two[0])
            weights = [upper]
        else:
            for done, pair in enumerate(waiting):
                in_grad = place_call(lambda a, b: a[...] + b[...], done, ROUNDS, pair, in_grad)
            weight = average_call(early_parts, 0, two[0], depth, None)
            weight = average_call(parts, two[0], depth, depth, weight)
    return (weight[None, None], moment[None, None], in_grad)


def solution(mesh):
    return jax.shard_map(
        on_device,
        mesh=mesh,
        in_specs=(
            P(None, ("expert", "node"), None),
            P(None, ("expert", "node")),
            P(None, ("expert", "node"), None),
            P("node", "expert", None, None),
            P("node", "expert", None, None),
        ),
        out_specs=(
            P("node", "expert", None, None),
            P("node", "expert", None, None),
            P(None, ("expert", "node"), None),
        ),
        check_vma=False,
    )
```

```python
import math

import jax
import jax.numpy as jnp
from jax import lax
from jax.experimental import pallas as pl
from jax.experimental.pallas import tpu as pltpu
from jax.sharding import PartitionSpec as P


ROUNDS = 2
NS_STEPS = 3
LEAD, LINEAR, QUADRATIC = 3.4445, -4.775, 2.0315
F32 = jnp.float32
BF16 = jnp.bfloat16
VMEM = pl.BlockSpec(memory_space=pltpu.VMEM)
SMEM = pl.BlockSpec(memory_space=pltpu.SMEM)
ANY = pl.BlockSpec(memory_space=pl.ANY)


def limit(mebibytes):
    return pltpu.CompilerParams(vmem_limit_bytes=mebibytes << 20)


def swapped(block, axis, bit):
    return lax.ppermute(block, axis, [(i, i ^ bit) for i in range(lax.axis_size(axis))])


def crossed(block, axis, way):
    count = lax.axis_size(axis)
    return lax.ppermute(
        block, axis, [((i + (-way if i % 2 else way)) % count, i) for i in range(count)]
    )


def dot(a, b):
    return jnp.dot(a, b, preferred_element_type=F32)


def dot_first(a, b):
    return lax.dot_general(a, b, (((0,), (0,)), ((), ())), preferred_element_type=F32)


def dot_last(a, b):
    return lax.dot_general(a, b, (((1,), (1,)), ((), ())), preferred_element_type=F32)


def joined(top, corner):
    edge = top.shape[0]
    below = jnp.concatenate([top[:, edge:].T, corner], axis=1)
    return jnp.concatenate([top, below], axis=0)


def product(left, right):
    edge = left.shape[0] // 2
    return dot(left[:edge], right), dot(left[edge:], right[:, edge:])


def low(pair):
    return tuple(item.astype(BF16) for item in pair)


def mix(*terms):
    return tuple(
        sum(factor * pair[i].astype(F32) for factor, pair in terms) for i in range(2)
    )


def factors(gram):
    rest, lead = None, 1.0
    for sweep in range(NS_STEPS):
        whole = joined(*gram)
        polynom_wide = mix((LINEAR, gram), (QUADRATIC, product(whole, whole)))
        polynom = joined(*low(polynom_wide))
        if sweep == 0:
            rest = polynom_wide
        else:
            rest = mix(
                (lead, polynom_wide), (LEAD, rest), (1.0, product(joined(*low(rest)), polynom))
            )
        lead = lead * LEAD
        if sweep < NS_STEPS - 1:
            half = low(mix((LEAD, gram), (1.0, product(whole, polynom))))
            gram = low(mix((LEAD, half), (1.0, product(joined(*half), polynom))))
    return joined(*low(rest))


def take(refs, start, stop, columns=slice(None)):
    parts, offset = [], 0
    for ref in refs:
        begin, end = max(start, offset), min(stop, offset + ref.shape[0])
        if begin < end:
            parts.append(ref[begin - offset : end - offset, columns])
        offset += ref.shape[0]
    return parts[0] if len(parts) == 1 else jnp.concatenate(parts, axis=0)


def put(refs, start, value):
    offset, stop = 0, start + value.shape[0]
    for ref in refs:
        begin, end = max(start, offset), min(stop, offset + ref.shape[0])
        if begin < end:
            ref[begin - offset : end - offset, :] = value[begin - start : end - start, :]
        offset += ref.shape[0]


def mixed(parts, start, stop):
    stepped, first, second, near = (take(refs, start, stop) for refs in parts)
    total = first.astype(F32) + second.astype(F32) + near.astype(F32)
    return 0.4 * stepped + 0.15 * total


def split(depth):
    half, unit = depth // 2, depth // 16
    return (half, half - 2 * unit, 2 * unit), (12 * unit, 4 * unit)


def sizes_of(arrays):
    return [len(item) for item in arrays]


def grouped(names, sizes):
    return [[next(names) for _ in range(size)] for size in sizes]


def ahead_kernel(sizes, refs):
    names = iter(refs)
    rows, parts = grouped(names, sizes[:1])[0], grouped(names, sizes[1:])
    if len(parts) == 1:
        value = parts[0][0][...]
    else:
        weight = next(names)
        value = mixed(parts, 0, weight.shape[0])
        weight[...] = value
    pre = next(names)
    shaped = value.astype(BF16)
    pre[...] = dot(take(rows, 0, pre.shape[0], slice(0, value.shape[0])), shaped)


def ahead_call(rows, parts, early):
    width = parts[0][0].shape[1]
    total = sum(item.shape[0] for item in rows)
    flat = [item for part in parts for item in part]
    shapes = [jax.ShapeDtypeStruct((total, width), F32)]
    if len(parts) > 1:
        shapes.insert(0, jax.ShapeDtypeStruct((early, width), F32))
    sizes = sizes_of([rows] + parts)
    return pl.pallas_call(
        lambda *refs: ahead_kernel(sizes, refs),
        out_shape=shapes,
        in_specs=[VMEM] * (len(rows) + len(flat)),
        out_specs=[VMEM] * len(shapes),
        compiler_params=limit(16),
        name="ahead",
    )(*rows, *flat)


def slope_rows(grads, place, value, slopes):
    width = slopes.shape[1]
    columns = slice(place, place + width)
    grad = take(grads, 0, slopes.shape[0], columns).astype(F32)
    slopes[...] = (grad * 2.0 * jnp.maximum(value, 0.0)).astype(BF16)


def weight_gradient(rows, slopes, span):
    return dot_first(take(rows, 0, slopes.shape[0], span), slopes[...])


def tiles(depth):
    tile = min(256, depth)
    return [slice(start, start + tile) for start in range(0, depth, tile)]


def part_kernel(sizes, refs):
    names = iter(refs)
    weight, moment = next(names), next(names)
    rows, grads = grouped(names, sizes)
    partial, slopes = names
    depth = moment.shape[0]
    factor = 1.0 / math.sqrt(depth)
    value = dot(take(rows, 0, slopes.shape[0]), weight[...].astype(BF16)) * factor
    slope_rows(grads, 0, value, slopes)
    for span in tiles(depth):
        partial[span, :] = 0.9 * moment[span, :] + weight_gradient(rows, slopes, span) * factor


def part_call(rows, grads, weight, moment):
    depth, width = moment.shape
    total = sum(item.shape[0] for item in rows)
    sizes = sizes_of([rows, grads])
    return pl.pallas_call(
        lambda *refs: part_kernel(sizes, refs),
        out_shape=[
            jax.ShapeDtypeStruct((depth, width), F32),
            jax.ShapeDtypeStruct((total, width), BF16),
        ],
        in_specs=[VMEM] * (2 + sum(sizes)),
        out_specs=[VMEM] * 2,
        compiler_params=limit(16),
        name="part_rows",
    )(weight, moment, *rows, *grads)


def round_kernel(sizes, place, decay, refs):
    names = iter(refs)
    pre, moment = next(names), next(names)
    rows, grads, weights, *parts = grouped(names, sizes)
    moment_out, slopes, moment_low, rest_out, scale_out, stepped, share = (
        next(names) for _ in range(7)
    )
    depth, width = moment.shape
    half, early = split(depth)[0][0], split(depth)[1][0]
    factor = 1.0 / math.sqrt(depth)
    if parts:
        late = next(names)
        value = mixed(parts, early, depth)
        late[...] = value
        shaped = value.astype(BF16)

    value = pre[...]
    if parts:
        value = value + dot(take(rows, 0, pre.shape[0], slice(early, depth)), shaped)
    slope_rows(grads, place, value * factor, slopes)
    total = jnp.zeros((1, width), F32)
    for span in tiles(depth):
        value = weight_gradient(rows, slopes, span) * factor
        value = (moment[span, :] if decay == 1.0 else decay * moment[span, :]) + value
        moment_out[span, :] = value
        moment_low[span, :] = value.astype(BF16)
        total = total + jnp.sum(value * value, axis=0, keepdims=True)
    scale = 1.0 / (jnp.sqrt(jnp.sum(total)) + 1e-07)
    scale_out[0] = scale
    edge = width // 2
    top = dot_first(moment_low[:, :edge], moment_low[...]) * (scale * scale)
    corner = dot_first(moment_low[:, edge:], moment_low[:, edge:]) * (scale * scale)
    rest = factors(low((top, corner)))
    rest_out[...] = rest
    step_rows(tiles(half), weights, moment_low, rest, scale, [stepped], [[share]], 0)


def step_rows(spans, weights, moment_low, rest, scale, stepped, shares, base):
    step_size = 0.1 * math.sqrt(moment_low.shape[0])
    for span in spans:
        low = moment_low[span, :]
        orthog = scale * (LEAD**NS_STEPS * low.astype(F32) + dot(low, rest))
        value = take(weights, span.start, span.stop) - step_size * orthog
        put(stepped, span.start - base, value)
        for refs in shares:
            put(refs, span.start - base, value.astype(BF16))


def round_call(rows, grads, place, decay, pre, weights, moment, parts):
    depth, width = moment.shape
    total = sum(item.shape[0] for item in rows)
    half, late = split(depth)[0][0], split(depth)[1][1]
    shape = jax.ShapeDtypeStruct
    flat = [item for part in parts for item in part]
    sizes = sizes_of([rows, grads, weights] + parts)
    out = [
        shape((depth, width), F32),
        shape((total, width), BF16),
        shape((depth, width), BF16),
        shape((width, width), BF16),
        shape((1,), F32),
        shape((half, width), F32),
        shape((half, width), BF16),
    ]
    specs = [VMEM] * 4 + [SMEM] + [VMEM] * 2
    if parts:
        out.append(shape((late, width), F32))
        specs.append(VMEM)
    return pl.pallas_call(
        lambda *refs: round_kernel(sizes, place, decay, refs),
        out_shape=out,
        in_specs=[VMEM] * (2 + sum(sizes)),
        out_specs=specs,
        compiler_params=limit(16),
        name="muon_round",
    )(pre, moment, *rows, *grads, *weights, *flat)


def second_kernel(count, refs):
    moment_low, rest, scale, share, *names = refs
    weights, names = names[:count], iter(names[count:])
    stepped, *rest_out = names
    ones, twos = rest_out[:2], rest_out[2:]
    depth = moment_low.shape[0]
    half = share.shape[0]
    put(twos, 0, share[...])
    spans = [span for span in tiles(depth) if span.start >= half]
    step_rows(spans, weights, moment_low, rest[...], scale[0], [stepped], [ones], half)
    put(twos, half, take(ones, 0, depth - half))


def second_call(moment_low, rest, scale, share, weights):
    depth, width = moment_low.shape
    one, two = split(depth)
    shape = jax.ShapeDtypeStruct
    out = [shape((depth - one[0], width), F32)]
    out = out + [shape((size, width), BF16) for size in one[1:] + two]
    result = pl.pallas_call(
        lambda *refs: second_kernel(len(weights), refs),
        out_shape=out,
        in_specs=[VMEM] * 2 + [SMEM] + [VMEM] * (1 + len(weights)),
        out_specs=[VMEM] * len(out),
        compiler_params=limit(12),
        name="second_half",
    )(moment_low, rest, scale, share, *weights)
    return result[0], [share, *result[1:3]], result[3:]


def picked(route, experts):
    count = route.shape[1]
    slots = count // 2
    lines = -(-experts // 8) * 8
    labels = lax.broadcasted_iota(jnp.int32, (lines, count), 0)
    keep = (route == labels).astype(F32)
    before = lax.broadcasted_iota(jnp.int32, (count, count), 0)
    after = lax.broadcasted_iota(jnp.int32, (count, count), 1)
    rank = dot(keep.astype(BF16), (before <= after).astype(BF16)) * keep
    slot = (lax.broadcasted_iota(jnp.int32, (slots, count), 0) + 1).astype(F32)
    return jnp.concatenate([slot == rank[m : m + 1, :] for m in range(experts)]).astype(BF16)


def squeeze_kernel(index, experts, fresh, count, refs):
    first, *refs = refs
    sources, outs = refs[:count], refs[count:]
    if fresh:
        picks, *outs = outs
        hot = picked(first[index : index + 1, :], experts)
        picks[...] = hot
    else:
        hot = first[...]
    slots = hot.shape[0] // experts
    place = 0
    for source in sources:
        value = dot(hot, source[0]).astype(BF16)
        for m, out in enumerate(outs):
            out[:, place : place + value.shape[1]] = value[m * slots : (m + 1) * slots, :]
        place += value.shape[1]


def squeeze_call(index, first, sources, experts, fresh):
    count = sources[0].shape[1]
    slots = count // 2
    width = sum(item.shape[2] for item in sources)
    shape = jax.ShapeDtypeStruct
    outs = [shape((slots, width), BF16)] * experts
    if fresh:
        outs.insert(0, shape((experts * slots, count), BF16))

    def whole(item):
        return pl.BlockSpec(item.shape, lambda i: (0, 0))

    return pl.pallas_call(
        lambda *refs: squeeze_kernel(index, experts, fresh, len(sources), refs),
        grid=(1,),
        out_shape=outs,
        in_specs=[whole(first)]
        + [pl.BlockSpec((1,) + item.shape[1:], lambda i: (index, 0, 0)) for item in sources],
        out_specs=[whole(item) for item in outs],
        compiler_params=limit(16),
        name="squeeze",
    )(first, *sources)


def backward_kernel(sizes, where, refs):
    names = iter(refs)
    slopes, weights = grouped(names, sizes)
    outs = list(names)
    count, depth = outs[0].shape
    factor = 1.0 / math.sqrt(depth)
    shaped = take(weights, 0, depth).astype(BF16)
    for out, (array, place) in zip(outs, where):
        part = slopes[array][place * count : (place + 1) * count, :]
        out[...] = (dot_last(part, shaped) * factor).astype(BF16)


def backward_call(slopes, weights, where, count):
    depth = sum(item.shape[0] for item in weights)
    sizes = sizes_of([slopes, weights])
    return pl.pallas_call(
        lambda *refs: backward_kernel(sizes, where, refs),
        out_shape=[jax.ShapeDtypeStruct((count, depth), BF16)] * len(where),
        in_specs=[VMEM] * sum(sizes),
        out_specs=[VMEM] * len(where),
        compiler_params=limit(16),
        name="row_gradients",
    )(*slopes, *weights)


def average_call(parts, start, stop, depth, buffer):
    flat = [item for part in parts for item in part]
    sizes = sizes_of(parts)
    extra = [] if buffer is None else [buffer]
    width = flat[0].shape[1]

    def kernel(*refs):
        names = iter(refs)
        groups = grouped(names, sizes)
        out, value, sem = list(names)[len(extra) :]
        value[...] = mixed(groups, start, stop)
        made = pltpu.make_async_copy(value, out.at[pl.ds(start, stop - start), :], sem)
        made.start()
        made.wait()

    return pl.pallas_call(
        kernel,
        out_shape=jax.ShapeDtypeStruct((depth, width), F32),
        in_specs=[VMEM] * len(flat) + [ANY] * len(extra),
        out_specs=ANY,
        scratch_shapes=[pltpu.VMEM((stop - start, width), F32), pltpu.SemaphoreType.DMA(())],
        input_output_aliases={len(flat): 0} if extra else {},
        compiler_params=limit(12),
        name="average",
    )(*flat, *extra)


def finish_call(index, picks, backs, buffer):
    count, depth = picks.shape[1], backs[0].shape[1]
    extra = [] if buffer is None else [buffer]

    def kernel(*refs):
        rows = take(refs[1 : 1 + len(backs)], 0, refs[0].shape[0])
        refs[-1][0] = dot_first(refs[0][...], rows).astype(BF16)

    def whole(item):
        return pl.BlockSpec(item.shape, lambda i: (0, 0))

    return pl.pallas_call(
        kernel,
        grid=(1,),
        out_shape=jax.ShapeDtypeStruct((ROUNDS, count, depth), BF16),
        in_specs=[whole(item) for item in (picks, *backs)] + [ANY] * len(extra),
        out_specs=pl.BlockSpec((1, count, depth), lambda i: (index, 0, 0)),
        input_output_aliases={1 + len(backs): 0} if extra else {},
        compiler_params=limit(12),
        name="finish",
    )(picks, *backs, *extra)


def on_device(tokens, routing, out_grad, weights, momentum):
    experts = lax.axis_size("expert")
    weight = weights[0, 0]
    moment = momentum[0, 0]
    depth = weight.shape[0]
    _, two = split(depth)
    slots = tokens.shape[1] // 2
    route = routing ^ lax.axis_index("expert").astype(jnp.int32)

    def exchanged(items):
        got = [items[0]]
        for m in range(1, experts):
            got.append(swapped(items[m], "expert", m))
        return got

    in_grad = None
    waiting = []
    picks, *items = squeeze_call(0, route, [tokens], experts, True)
    all_picks = [picks]
    rows = exchanged(items)
    items = squeeze_call(0, picks, [out_grad], experts, False)
    grads = exchanged(items)
    picks, *items = squeeze_call(1, route, [tokens, out_grad], experts, True)
    all_picks.append(picks)
    later = exchanged(items)
    moment, slopes = part_call(rows[:2], grads[:2], weight, moment)
    all_slopes = [slopes]
    (pre,) = ahead_call(rows[2:], [[weight]], depth)
    where = [
        [(m // 2, m) if m < 2 else (1, m - 2) for m in range(experts)],
        [(0, m) for m in range(experts)],
    ]
    weights = [weight]
    parts = []
    for index in range(ROUNDS):
        if index:
            moment, slopes, low, rest, scale, stepped, share, late = round_call(
                later, later, depth, 0.9, pre, weights, moment, parts
            )
            weights = [*weights, late]
            all_slopes = [slopes]
        else:
            moment, slopes, low, rest, scale, stepped, share = round_call(
                rows[2:], grads[2:], 0, 1.0, pre, weights, moment, parts
            )
            all_slopes.append(slopes)
        stepped_low, ones, twos = second_call(low, rest, scale, share, weights)
        firsts = []
        for item in ones:
            firsts.append(crossed(item, "node", 2))
        seconds = []
        for item in twos:
            seconds.append(crossed(item, "node", -2))
        nears = []
        got = [firsts[0], jnp.concatenate(firsts[1:])]
        for piece, item in enumerate((share, jnp.concatenate(ones[1:]))):
            pair = (item.astype(F32) + got[piece].astype(F32)).astype(BF16)
            nears.append(swapped(pair, "node", 1))
        far = backward_call(all_slopes, weights, where[index][2:], slots)
        near = backward_call(all_slopes, weights, where[index][:2], slots)
        waiting.append(exchanged([*near, *far]))
        halves = [stepped, stepped_low]
        parts = [halves, firsts, seconds, nears]
        early_parts = [halves, firsts[:2], seconds[:1], nears[:2]]
        if index < ROUNDS - 1:
            upper, pre = ahead_call(later, early_parts, two[0])
            weights = [upper]
        else:
            for done, backs in enumerate(waiting):
                in_grad = finish_call(done, all_picks[done], backs, in_grad)
            weight = average_call(early_parts, 0, two[0], depth, None)
            weight = average_call(parts, two[0], depth, depth, weight)
    return (weight[None, None], moment[None, None], in_grad)


def solution(mesh):
    return jax.shard_map(
        on_device,
        mesh=mesh,
        in_specs=(
            P(None, ("expert", "node"), None),
            P(None, ("expert", "node")),
            P(None, ("expert", "node"), None),
            P("node", "expert", None, None),
            P("node", "expert", None, None),
        ),
        out_specs=(
            P("node", "expert", None, None),
            P("node", "expert", None, None),
            P(None, ("expert", "node"), None),
        ),
        check_vma=False,
    )
```

```python
import math

import jax
import jax.numpy as jnp
from jax import lax
from jax.experimental import pallas as pl
from jax.experimental.pallas import tpu as pltpu
from jax.sharding import PartitionSpec as P


ROUNDS = 2
NS_STEPS = 3
LEAD, LINEAR, QUADRATIC = 3.4445, -4.775, 2.0315
F32 = jnp.float32
BF16 = jnp.bfloat16
VMEM = pl.BlockSpec(memory_space=pltpu.VMEM)
SMEM = pl.BlockSpec(memory_space=pltpu.SMEM)
ANY = pl.BlockSpec(memory_space=pl.ANY)


def limit(mebibytes):
    return pltpu.CompilerParams(vmem_limit_bytes=mebibytes << 20)


def swapped(block, axis, bit):
    return lax.ppermute(block, axis, [(i, i ^ bit) for i in range(lax.axis_size(axis))])


def crossed(block, axis, way):
    count = lax.axis_size(axis)
    return lax.ppermute(
        block, axis, [((i + (-way if i % 2 else way)) % count, i) for i in range(count)]
    )


def dot(a, b):
    return jnp.dot(a, b, preferred_element_type=F32)


def dot_first(a, b):
    return lax.dot_general(a, b, (((0,), (0,)), ((), ())), preferred_element_type=F32)


def dot_last(a, b):
    return lax.dot_general(a, b, (((1,), (1,)), ((), ())), preferred_element_type=F32)


def joined(top, corner):
    edge = top.shape[0]
    below = jnp.concatenate([top[:, edge:].T, corner], axis=1)
    return jnp.concatenate([top, below], axis=0)


def product(left, right):
    edge = left.shape[0] // 2
    return dot(left[:edge], right), dot(left[edge:], right[:, edge:])


def low(pair):
    return tuple(item.astype(BF16) for item in pair)


def mix(*terms):
    return tuple(
        sum(factor * pair[i].astype(F32) for factor, pair in terms) for i in range(2)
    )


def factors(gram):
    rest, lead = None, 1.0
    for sweep in range(NS_STEPS):
        whole = joined(*gram)
        polynom_wide = mix((LINEAR, gram), (QUADRATIC, product(whole, whole)))
        polynom = joined(*low(polynom_wide))
        if sweep == 0:
            rest = polynom_wide
        else:
            rest = mix(
                (lead, polynom_wide), (LEAD, rest), (1.0, product(joined(*low(rest)), polynom))
            )
        lead = lead * LEAD
        if sweep < NS_STEPS - 1:
            half = low(mix((LEAD, gram), (1.0, product(whole, polynom))))
            gram = low(mix((LEAD, half), (1.0, product(joined(*half), polynom))))
    return joined(*low(rest))


def take(refs, start, stop, columns=slice(None)):
    parts, offset = [], 0
    for ref in refs:
        begin, end = max(start, offset), min(stop, offset + ref.shape[0])
        if begin < end:
            parts.append(ref[begin - offset : end - offset, columns])
        offset += ref.shape[0]
    return parts[0] if len(parts) == 1 else jnp.concatenate(parts, axis=0)


def put(refs, start, value):
    offset, stop = 0, start + value.shape[0]
    for ref in refs:
        begin, end = max(start, offset), min(stop, offset + ref.shape[0])
        if begin < end:
            ref[begin - offset : end - offset, :] = value[begin - start : end - start, :]
        offset += ref.shape[0]


def mixed(parts, start, stop):
    stepped, first, second, near = (take(refs, start, stop) for refs in parts)
    total = first.astype(F32) + second.astype(F32) + near.astype(F32)
    return 0.4 * stepped + 0.15 * total


def split(depth):
    half, unit = depth // 2, depth // 16
    return (half // 2, 3 * half // 2 - 2 * unit, 2 * unit), (12 * unit, 4 * unit)


def sizes_of(arrays):
    return [len(item) for item in arrays]


def grouped(names, sizes):
    return [[next(names) for _ in range(size)] for size in sizes]


def ahead_kernel(sizes, refs):
    names = iter(refs)
    rows, parts = grouped(names, sizes[:1])[0], grouped(names, sizes[1:])
    if len(parts) == 1:
        value = parts[0][0][...]
    else:
        weight = next(names)
        value = mixed(parts, 0, weight.shape[0])
        weight[...] = value
    pre = next(names)
    shaped = value.astype(BF16)
    pre[...] = dot(take(rows, 0, pre.shape[0], slice(0, value.shape[0])), shaped)


def ahead_call(rows, parts, early):
    width = parts[0][0].shape[1]
    total = sum(item.shape[0] for item in rows)
    flat = [item for part in parts for item in part]
    shapes = [jax.ShapeDtypeStruct((total, width), F32)]
    if len(parts) > 1:
        shapes.insert(0, jax.ShapeDtypeStruct((early, width), F32))
    sizes = sizes_of([rows] + parts)
    return pl.pallas_call(
        lambda *refs: ahead_kernel(sizes, refs),
        out_shape=shapes,
        in_specs=[VMEM] * (len(rows) + len(flat)),
        out_specs=[VMEM] * len(shapes),
        compiler_params=limit(16),
        name="ahead",
    )(*rows, *flat)


def slope_rows(grads, place, value, slopes):
    width = slopes.shape[1]
    columns = slice(place, place + width)
    grad = take(grads, 0, slopes.shape[0], columns).astype(F32)
    slopes[...] = (grad * 2.0 * jnp.maximum(value, 0.0)).astype(BF16)


def weight_gradient(rows, slopes, span):
    return dot_first(take(rows, 0, slopes.shape[0], span), slopes[...])


def tiles(depth):
    tile = min(256, depth)
    return [slice(start, start + tile) for start in range(0, depth, tile)]


def part_kernel(sizes, refs):
    names = iter(refs)
    weight, moment = next(names), next(names)
    rows, grads = grouped(names, sizes)
    partial, slopes = names
    depth = moment.shape[0]
    factor = 1.0 / math.sqrt(depth)
    value = dot(take(rows, 0, slopes.shape[0]), weight[...].astype(BF16)) * factor
    slope_rows(grads, 0, value, slopes)
    for span in tiles(depth):
        partial[span, :] = 0.9 * moment[span, :] + weight_gradient(rows, slopes, span) * factor


def part_call(rows, grads, weight, moment):
    depth, width = moment.shape
    total = sum(item.shape[0] for item in rows)
    sizes = sizes_of([rows, grads])
    return pl.pallas_call(
        lambda *refs: part_kernel(sizes, refs),
        out_shape=[
            jax.ShapeDtypeStruct((depth, width), F32),
            jax.ShapeDtypeStruct((total, width), BF16),
        ],
        in_specs=[VMEM] * (2 + sum(sizes)),
        out_specs=[VMEM] * 2,
        compiler_params=limit(16),
        name="part_rows",
    )(weight, moment, *rows, *grads)


def round_kernel(sizes, place, decay, refs):
    names = iter(refs)
    pre, moment = next(names), next(names)
    rows, grads, weights, *parts = grouped(names, sizes)
    moment_out, slopes, moment_low, rest_out, scale_out, stepped, share = (
        next(names) for _ in range(7)
    )
    depth, width = moment.shape
    half, early = split(depth)[0][0], split(depth)[1][0]
    factor = 1.0 / math.sqrt(depth)
    if parts:
        late = next(names)
        value = mixed(parts, early, depth)
        late[...] = value
        shaped = value.astype(BF16)

    value = pre[...]
    if parts:
        value = value + dot(take(rows, 0, pre.shape[0], slice(early, depth)), shaped)
    slope_rows(grads, place, value * factor, slopes)
    total = jnp.zeros((1, width), F32)
    for span in tiles(depth):
        value = weight_gradient(rows, slopes, span) * factor
        value = (moment[span, :] if decay == 1.0 else decay * moment[span, :]) + value
        moment_out[span, :] = value
        moment_low[span, :] = value.astype(BF16)
        total = total + jnp.sum(value * value, axis=0, keepdims=True)
    scale = 1.0 / (jnp.sqrt(jnp.sum(total)) + 1e-07)
    scale_out[0] = scale
    edge = width // 2
    top = dot_first(moment_low[:, :edge], moment_low[...]) * (scale * scale)
    corner = dot_first(moment_low[:, edge:], moment_low[:, edge:]) * (scale * scale)
    rest = factors(low((top, corner)))
    rest_out[...] = rest
    step_rows(tiles(half), weights, moment_low, rest, scale, [stepped], [[share]], 0)


def step_rows(spans, weights, moment_low, rest, scale, stepped, shares, base):
    step_size = 0.1 * math.sqrt(moment_low.shape[0])
    for span in spans:
        low = moment_low[span, :]
        orthog = scale * (LEAD**NS_STEPS * low.astype(F32) + dot(low, rest))
        value = take(weights, span.start, span.stop) - step_size * orthog
        put(stepped, span.start - base, value)
        for refs in shares:
            put(refs, span.start - base, value.astype(BF16))


def round_call(rows, grads, place, decay, pre, weights, moment, parts):
    depth, width = moment.shape
    total = sum(item.shape[0] for item in rows)
    half, late = split(depth)[0][0], split(depth)[1][1]
    shape = jax.ShapeDtypeStruct
    flat = [item for part in parts for item in part]
    sizes = sizes_of([rows, grads, weights] + parts)
    out = [
        shape((depth, width), F32),
        shape((total, width), BF16),
        shape((depth, width), BF16),
        shape((width, width), BF16),
        shape((1,), F32),
        shape((half, width), F32),
        shape((half, width), BF16),
    ]
    specs = [VMEM] * 4 + [SMEM] + [VMEM] * 2
    if parts:
        out.append(shape((late, width), F32))
        specs.append(VMEM)
    return pl.pallas_call(
        lambda *refs: round_kernel(sizes, place, decay, refs),
        out_shape=out,
        in_specs=[VMEM] * (2 + sum(sizes)),
        out_specs=specs,
        compiler_params=limit(16),
        name="muon_round",
    )(pre, moment, *rows, *grads, *weights, *flat)


def second_kernel(count, refs):
    moment_low, rest, scale, share, *names = refs
    weights, names = names[:count], iter(names[count:])
    stepped, *rest_out = names
    ones, twos = rest_out[:2], rest_out[2:]
    depth = moment_low.shape[0]
    half = share.shape[0]
    put(twos, 0, share[...])
    spans = [span for span in tiles(depth) if span.start >= half]
    step_rows(spans, weights, moment_low, rest[...], scale[0], [stepped], [ones], half)
    put(twos, half, take(ones, 0, depth - half))


def second_call(moment_low, rest, scale, share, weights):
    depth, width = moment_low.shape
    one, two = split(depth)
    shape = jax.ShapeDtypeStruct
    out = [shape((depth - one[0], width), F32)]
    out = out + [shape((size, width), BF16) for size in one[1:] + two]
    result = pl.pallas_call(
        lambda *refs: second_kernel(len(weights), refs),
        out_shape=out,
        in_specs=[VMEM] * 2 + [SMEM] + [VMEM] * (1 + len(weights)),
        out_specs=[VMEM] * len(out),
        compiler_params=limit(12),
        name="second_half",
    )(moment_low, rest, scale, share, *weights)
    return result[0], [share, *result[1:3]], result[3:]


def picked(route, mine, experts):
    count = route.shape[1]
    slots = count // 2
    lines = -(-experts // 8) * 8
    labels = lax.broadcasted_iota(jnp.int32, (lines, count), 0) ^ mine
    keep = (route == labels).astype(F32)
    before = lax.broadcasted_iota(jnp.int32, (count, count), 0)
    after = lax.broadcasted_iota(jnp.int32, (count, count), 1)
    rank = dot(keep.astype(BF16), (before <= after).astype(BF16)) * keep
    slot = (lax.broadcasted_iota(jnp.int32, (slots, count), 0) + 1).astype(F32)
    return jnp.concatenate([slot == rank[m : m + 1, :] for m in range(experts)]).astype(BF16)


def picks_kernel(experts, far, route_ref, mine, tokens_ref, *refs):
    outs, (route, tokens, sems) = refs[:-3], refs[-3:]
    made = [
        pltpu.make_async_copy(route_ref, route, sems.at[0]),
        pltpu.make_async_copy(tokens_ref.at[0], tokens, sems.at[1]),
    ]
    for item in made:
        item.start()
    made[0].wait()
    picks, outs = outs[: route.shape[0]], outs[route.shape[0] :]
    hot = None
    for index, out in enumerate(picks):
        value = picked(route[index : index + 1, :], mine[0], experts)
        out[...] = value
        hot = value if hot is None else hot
    made[1].wait()
    slots = hot.shape[0] // experts
    for m, out in zip(far, outs):
        out[...] = dot(hot[m * slots : (m + 1) * slots], tokens[...]).astype(BF16)


def picks_call(routing, mine, tokens, experts, far):
    rounds, count, depth = tokens.shape
    shape = jax.ShapeDtypeStruct
    slots = count // 2
    outs = [shape((experts * slots, count), BF16)] * rounds + [shape((slots, depth), BF16)] * len(far)
    result = pl.pallas_call(
        lambda *refs: picks_kernel(experts, far, *refs),
        out_shape=outs,
        in_specs=[ANY, SMEM, ANY],
        out_specs=[VMEM] * len(outs),
        scratch_shapes=[
            pltpu.VMEM((rounds, count), jnp.int32),
            pltpu.VMEM((count, depth), BF16),
            pltpu.SemaphoreType.DMA((2,)),
        ],
        compiler_params=limit(52),
        name="picks",
    )(routing, mine, tokens)
    return result[:rounds], result[rounds:]


def squeeze_kernel(count, chosen, experts, refs):
    picks, sources, outs = refs[0], refs[1 : 1 + count], refs[1 + count :]
    slots = picks.shape[0] // experts
    hot = picks[: (max(chosen) + 1) * slots, :]
    place = 0
    for source in sources:
        value = dot(hot, source[0]).astype(BF16)
        for m, out in zip(chosen, outs):
            out[:, place : place + value.shape[1]] = value[m * slots : (m + 1) * slots, :]
        place += value.shape[1]


def squeeze_call(index, picks, sources, chosen, experts):
    width = sum(item.shape[2] for item in sources)
    outs = [jax.ShapeDtypeStruct((picks.shape[0] // experts, width), BF16)] * len(chosen)

    def whole(item):
        return pl.BlockSpec(item.shape, lambda i: (0, 0))

    return pl.pallas_call(
        lambda *refs: squeeze_kernel(len(sources), chosen, experts, refs),
        grid=(1,),
        out_shape=outs,
        in_specs=[whole(picks)]
        + [pl.BlockSpec((1,) + item.shape[1:], lambda i: (index, 0, 0)) for item in sources],
        out_specs=[whole(item) for item in outs],
        compiler_params=limit(16),
        name="squeeze",
    )(picks, *sources)


def backward_kernel(sizes, where, refs):
    names = iter(refs)
    slopes, weights = grouped(names, sizes)
    outs = list(names)
    count, depth = outs[0].shape
    factor = 1.0 / math.sqrt(depth)
    shaped = take(weights, 0, depth).astype(BF16)
    for out, (array, place) in zip(outs, where):
        part = slopes[array][place * count : (place + 1) * count, :]
        out[...] = (dot_last(part, shaped) * factor).astype(BF16)


def backward_call(slopes, weights, where, count):
    depth = sum(item.shape[0] for item in weights)
    sizes = sizes_of([slopes, weights])
    return pl.pallas_call(
        lambda *refs: backward_kernel(sizes, where, refs),
        out_shape=[jax.ShapeDtypeStruct((count, depth), BF16)] * len(where),
        in_specs=[VMEM] * sum(sizes),
        out_specs=[VMEM] * len(where),
        compiler_params=limit(16),
        name="row_gradients",
    )(*slopes, *weights)


def average_call(parts, start, stop, depth, buffer):
    flat = [item for part in parts for item in part]
    sizes = sizes_of(parts)
    extra = [] if buffer is None else [buffer]
    width = flat[0].shape[1]

    def kernel(*refs):
        names = iter(refs)
        groups = grouped(names, sizes)
        out, value, sem = list(names)[len(extra) :]
        value[...] = mixed(groups, start, stop)
        made = pltpu.make_async_copy(value, out.at[pl.ds(start, stop - start), :], sem)
        made.start()
        made.wait()

    return pl.pallas_call(
        kernel,
        out_shape=jax.ShapeDtypeStruct((depth, width), F32),
        in_specs=[VMEM] * len(flat) + [ANY] * len(extra),
        out_specs=ANY,
        scratch_shapes=[pltpu.VMEM((stop - start, width), F32), pltpu.SemaphoreType.DMA(())],
        input_output_aliases={len(flat): 0} if extra else {},
        compiler_params=limit(12),
        name="average",
    )(*flat, *extra)


def finish_call(index, picks, backs, buffer):
    count, depth = picks.shape[1], backs[0].shape[1]
    extra = [] if buffer is None else [buffer]

    def kernel(*refs):
        rows = take(refs[1 : 1 + len(backs)], 0, refs[0].shape[0])
        refs[-1][0] = dot_first(refs[0][...], rows).astype(BF16)

    def whole(item):
        return pl.BlockSpec(item.shape, lambda i: (0, 0))

    return pl.pallas_call(
        kernel,
        grid=(1,),
        out_shape=jax.ShapeDtypeStruct((ROUNDS, count, depth), BF16),
        in_specs=[whole(item) for item in (picks, *backs)] + [ANY] * len(extra),
        out_specs=pl.BlockSpec((1, count, depth), lambda i: (index, 0, 0)),
        input_output_aliases={1 + len(backs): 0} if extra else {},
        compiler_params=limit(12),
        name="finish",
    )(picks, *backs, *extra)


def on_device(tokens, routing, out_grad, weights, momentum):
    experts = lax.axis_size("expert")
    weight = weights[0, 0]
    moment = momentum[0, 0]
    depth = weight.shape[0]
    _, two = split(depth)
    slots = tokens.shape[1] // 2
    mine = lax.axis_index("expert").astype(jnp.int32).reshape(1)

    def exchanged(items):
        got = [items[0]]
        for m in range(1, experts):
            got.append(swapped(items[m], "expert", m))
        return got

    in_grad = None
    waiting = []
    every, close = list(range(experts)), [0, 1]
    all_picks, items = picks_call(routing, mine, tokens, experts, every[2:])
    items = [*squeeze_call(0, all_picks[0], [tokens], close, experts), *items]
    rows = exchanged(items)
    items = squeeze_call(0, all_picks[0], [out_grad], every, experts)
    grads = exchanged(items)
    items = squeeze_call(1, all_picks[1], [tokens, out_grad], every, experts)
    later = exchanged(items)
    moment, slopes = part_call(rows[:2], grads[:2], weight, moment)
    all_slopes = [slopes]
    (pre,) = ahead_call(rows[2:], [[weight]], depth)
    where = [
        [(m // 2, m) if m < 2 else (1, m - 2) for m in range(experts)],
        [(0, m) for m in range(experts)],
    ]
    weights = [weight]
    parts = []
    for index in range(ROUNDS):
        if index:
            moment, slopes, low, rest, scale, stepped, share, late = round_call(
                later, later, depth, 0.9, pre, weights, moment, parts
            )
            weights = [*weights, late]
            all_slopes = [slopes]
        else:
            moment, slopes, low, rest, scale, stepped, share = round_call(
                rows[2:], grads[2:], 0, 1.0, pre, weights, moment, parts
            )
            all_slopes.append(slopes)
        stepped_low, ones, twos = second_call(low, rest, scale, share, weights)
        firsts = []
        for item in ones:
            firsts.append(crossed(item, "node", 2))
        seconds = []
        for item in twos:
            seconds.append(crossed(item, "node", -2))
        nears = []
        got = [firsts[0], jnp.concatenate(firsts[1:])]
        for piece, item in enumerate((share, jnp.concatenate(ones[1:]))):
            pair = (item.astype(F32) + got[piece].astype(F32)).astype(BF16)
            nears.append(swapped(pair, "node", 1))
        far = backward_call(all_slopes, weights, where[index][2:], slots)
        near = backward_call(all_slopes, weights, where[index][:2], slots)
        waiting.append(exchanged([*near, *far]))
        halves = [stepped, stepped_low]
        parts = [halves, firsts, seconds, nears]
        early_parts = [halves, firsts[:2], seconds[:1], nears[:2]]
        if index < ROUNDS - 1:
            upper, pre = ahead_call(later, early_parts, two[0])
            weights = [upper]
        else:
            for done, backs in enumerate(waiting):
                in_grad = finish_call(done, all_picks[done], backs, in_grad)
            weight = average_call(early_parts, 0, two[0], depth, None)
            weight = average_call(parts, two[0], depth, depth, weight)
    return (weight[None, None], moment[None, None], in_grad)


def solution(mesh):
    return jax.shard_map(
        on_device,
        mesh=mesh,
        in_specs=(
            P(None, ("expert", "node"), None),
            P(None, ("expert", "node")),
            P(None, ("expert", "node"), None),
            P("node", "expert", None, None),
            P("node", "expert", None, None),
        ),
        out_specs=(
            P("node", "expert", None, None),
            P("node", "expert", None, None),
            P(None, ("expert", "node"), None),
        ),
        check_vma=False,
    )
```

```python
import math

import jax
import jax.numpy as jnp
from jax import lax
from jax.experimental import pallas as pl
from jax.experimental.pallas import tpu as pltpu
from jax.sharding import PartitionSpec as P


ROUNDS = 2
NS_STEPS = 3
LEAD, LINEAR, QUADRATIC = 3.4445, -4.775, 2.0315
F32 = jnp.float32
BF16 = jnp.bfloat16
VMEM = pl.BlockSpec(memory_space=pltpu.VMEM)
SMEM = pl.BlockSpec(memory_space=pltpu.SMEM)
ANY = pl.BlockSpec(memory_space=pl.ANY)


def limit(mebibytes):
    return pltpu.CompilerParams(vmem_limit_bytes=mebibytes << 20)


def swapped(block, axis, bit):
    return lax.ppermute(block, axis, [(i, i ^ bit) for i in range(lax.axis_size(axis))])


def crossed(block, axis, way):
    count = lax.axis_size(axis)
    return lax.ppermute(
        block, axis, [((i + (-way if i % 2 else way)) % count, i) for i in range(count)]
    )


def dot(a, b):
    return jnp.dot(a, b, preferred_element_type=F32)


def dot_first(a, b):
    return lax.dot_general(a, b, (((0,), (0,)), ((), ())), preferred_element_type=F32)


def dot_last(a, b):
    return lax.dot_general(a, b, (((1,), (1,)), ((), ())), preferred_element_type=F32)


def joined(top, corner):
    edge = top.shape[0]
    below = jnp.concatenate([top[:, edge:].T, corner], axis=1)
    return jnp.concatenate([top, below], axis=0)


def product(left, right):
    edge = left.shape[0] // 2
    return dot(left[:edge], right), dot(left[edge:], right[:, edge:])


def low(pair):
    return tuple(item.astype(BF16) for item in pair)


def mix(*terms):
    return tuple(
        sum(factor * pair[i].astype(F32) for factor, pair in terms) for i in range(2)
    )


def factors(gram):
    rest, lead = None, 1.0
    for sweep in range(NS_STEPS):
        whole = joined(*gram)
        polynom_wide = mix((LINEAR, gram), (QUADRATIC, product(whole, whole)))
        polynom = joined(*low(polynom_wide))
        if sweep == 0:
            rest = polynom_wide
        else:
            rest = mix(
                (lead, polynom_wide), (LEAD, rest), (1.0, product(joined(*low(rest)), polynom))
            )
        lead = lead * LEAD
        if sweep < NS_STEPS - 1:
            half = low(mix((LEAD, gram), (1.0, product(whole, polynom))))
            gram = low(mix((LEAD, half), (1.0, product(joined(*half), polynom))))
    return joined(*low(rest))


def take(refs, start, stop, columns=slice(None)):
    parts, offset = [], 0
    for ref in refs:
        begin, end = max(start, offset), min(stop, offset + ref.shape[0])
        if begin < end:
            parts.append(ref[begin - offset : end - offset, columns])
        offset += ref.shape[0]
    return parts[0] if len(parts) == 1 else jnp.concatenate(parts, axis=0)


def put(refs, start, value):
    offset, stop = 0, start + value.shape[0]
    for ref in refs:
        begin, end = max(start, offset), min(stop, offset + ref.shape[0])
        if begin < end:
            ref[begin - offset : end - offset, :] = value[begin - start : end - start, :]
        offset += ref.shape[0]


def mixed(parts, start, stop):
    stepped, first, second, near = (take(refs, start, stop) for refs in parts)
    total = first.astype(F32) + second.astype(F32) + near.astype(F32)
    return 0.4 * stepped + 0.15 * total


def split(depth):
    half, unit = depth // 2, depth // 16
    return (half // 2, 3 * half // 2 - 2 * unit, 2 * unit), (12 * unit, 4 * unit)


def sizes_of(arrays):
    return [len(item) for item in arrays]


def grouped(names, sizes):
    return [[next(names) for _ in range(size)] for size in sizes]


def ahead_kernel(sizes, refs):
    names = iter(refs)
    rows, parts = grouped(names, sizes[:1])[0], grouped(names, sizes[1:])
    if len(parts) == 1:
        value = parts[0][0][...]
    else:
        weight = next(names)
        value = mixed(parts, 0, weight.shape[0])
        weight[...] = value
    pre = next(names)
    shaped = value.astype(BF16)
    pre[...] = dot(take(rows, 0, pre.shape[0], slice(0, value.shape[0])), shaped)


def ahead_call(rows, parts, early):
    width = parts[0][0].shape[1]
    total = sum(item.shape[0] for item in rows)
    flat = [item for part in parts for item in part]
    shapes = [jax.ShapeDtypeStruct((total, width), F32)]
    if len(parts) > 1:
        shapes.insert(0, jax.ShapeDtypeStruct((early, width), F32))
    sizes = sizes_of([rows] + parts)
    return pl.pallas_call(
        lambda *refs: ahead_kernel(sizes, refs),
        out_shape=shapes,
        in_specs=[VMEM] * (len(rows) + len(flat)),
        out_specs=[VMEM] * len(shapes),
        compiler_params=limit(16),
        name="ahead",
    )(*rows, *flat)


def slope_rows(grads, place, value, slopes):
    width = slopes.shape[1]
    columns = slice(place, place + width)
    grad = take(grads, 0, slopes.shape[0], columns).astype(F32)
    slopes[...] = (grad * 2.0 * jnp.maximum(value, 0.0)).astype(BF16)


def weight_gradient(rows, slopes, span):
    return dot_first(take(rows, 0, slopes.shape[0], span), slopes[...])


def tiles(depth):
    tile = min(256, depth)
    return [slice(start, start + tile) for start in range(0, depth, tile)]


def part_kernel(sizes, decay, refs):
    names = iter(refs)
    weight, moment = next(names), next(names)
    rows, grads = grouped(names, sizes)
    partial, slopes = names
    depth = moment.shape[0]
    factor = 1.0 / math.sqrt(depth)
    value = dot(take(rows, 0, slopes.shape[0]), weight[...].astype(BF16)) * factor
    slope_rows(grads, 0, value, slopes)
    for span in tiles(depth):
        before = moment[span, :] if decay == 1.0 else decay * moment[span, :]
        partial[span, :] = before + weight_gradient(rows, slopes, span) * factor


def part_call(rows, grads, weight, moment, decay):
    depth, width = moment.shape
    total = sum(item.shape[0] for item in rows)
    sizes = sizes_of([rows, grads])
    return pl.pallas_call(
        lambda *refs: part_kernel(sizes, decay, refs),
        out_shape=[
            jax.ShapeDtypeStruct((depth, width), F32),
            jax.ShapeDtypeStruct((total, width), BF16),
        ],
        in_specs=[VMEM] * (2 + sum(sizes)),
        out_specs=[VMEM] * 2,
        compiler_params=limit(16),
        name="part_rows",
    )(weight, moment, *rows, *grads)


def round_kernel(sizes, place, decay, refs):
    names = iter(refs)
    pre, moment = next(names), next(names)
    rows, grads, weights, *parts = grouped(names, sizes)
    moment_out, slopes, moment_low, rest_out, scale_out, stepped, share = (
        next(names) for _ in range(7)
    )
    depth, width = moment.shape
    half, early = split(depth)[0][0], split(depth)[1][0]
    factor = 1.0 / math.sqrt(depth)
    if parts:
        late = next(names)
        value = mixed(parts, early, depth)
        late[...] = value
        shaped = value.astype(BF16)

    value = pre[...]
    if parts:
        value = value + dot(take(rows, 0, pre.shape[0], slice(early, depth)), shaped)
    slope_rows(grads, place, value * factor, slopes)
    total = jnp.zeros((1, width), F32)
    for span in tiles(depth):
        value = weight_gradient(rows, slopes, span) * factor
        value = (moment[span, :] if decay == 1.0 else decay * moment[span, :]) + value
        moment_out[span, :] = value
        moment_low[span, :] = value.astype(BF16)
        total = total + jnp.sum(value * value, axis=0, keepdims=True)
    scale = 1.0 / (jnp.sqrt(jnp.sum(total)) + 1e-07)
    scale_out[0] = scale
    edge = width // 2
    top = dot_first(moment_low[:, :edge], moment_low[...]) * (scale * scale)
    corner = dot_first(moment_low[:, edge:], moment_low[:, edge:]) * (scale * scale)
    rest = factors(low((top, corner)))
    rest_out[...] = rest
    step_rows(tiles(half), weights, moment_low, rest, scale, [stepped], [[share]], 0)


def step_rows(spans, weights, moment_low, rest, scale, stepped, shares, base):
    step_size = 0.1 * math.sqrt(moment_low.shape[0])
    for span in spans:
        low = moment_low[span, :]
        orthog = scale * (LEAD**NS_STEPS * low.astype(F32) + dot(low, rest))
        value = take(weights, span.start, span.stop) - step_size * orthog
        put(stepped, span.start - base, value)
        for refs in shares:
            put(refs, span.start - base, value.astype(BF16))


def round_call(rows, grads, place, decay, pre, weights, moment, parts):
    depth, width = moment.shape
    total = sum(item.shape[0] for item in rows)
    half, late = split(depth)[0][0], split(depth)[1][1]
    shape = jax.ShapeDtypeStruct
    flat = [item for part in parts for item in part]
    sizes = sizes_of([rows, grads, weights] + parts)
    out = [
        shape((depth, width), F32),
        shape((total, width), BF16),
        shape((depth, width), BF16),
        shape((width, width), BF16),
        shape((1,), F32),
        shape((half, width), F32),
        shape((half, width), BF16),
    ]
    specs = [VMEM] * 4 + [SMEM] + [VMEM] * 2
    if parts:
        out.append(shape((late, width), F32))
        specs.append(VMEM)
    return pl.pallas_call(
        lambda *refs: round_kernel(sizes, place, decay, refs),
        out_shape=out,
        in_specs=[VMEM] * (2 + sum(sizes)),
        out_specs=specs,
        compiler_params=limit(16),
        name="muon_round",
    )(pre, moment, *rows, *grads, *weights, *flat)


def second_kernel(count, refs):
    moment_low, rest, scale, share, *names = refs
    weights, names = names[:count], iter(names[count:])
    stepped, *rest_out = names
    ones, twos = rest_out[:2], rest_out[2:]
    depth = moment_low.shape[0]
    half = share.shape[0]
    put(twos, 0, share[...])
    spans = [span for span in tiles(depth) if span.start >= half]
    step_rows(spans, weights, moment_low, rest[...], scale[0], [stepped], [ones], half)
    put(twos, half, take(ones, 0, depth - half))


def second_call(moment_low, rest, scale, share, weights):
    depth, width = moment_low.shape
    one, two = split(depth)
    shape = jax.ShapeDtypeStruct
    out = [shape((depth - one[0], width), F32)]
    out = out + [shape((size, width), BF16) for size in one[1:] + two]
    result = pl.pallas_call(
        lambda *refs: second_kernel(len(weights), refs),
        out_shape=out,
        in_specs=[VMEM] * 2 + [SMEM] + [VMEM] * (1 + len(weights)),
        out_specs=[VMEM] * len(out),
        compiler_params=limit(12),
        name="second_half",
    )(moment_low, rest, scale, share, *weights)
    return result[0], [share, *result[1:3]], result[3:]


def picked(route, mine, experts):
    count = route.shape[1]
    slots = count // 2
    lines = -(-experts // 8) * 8
    labels = lax.broadcasted_iota(jnp.int32, (lines, count), 0) ^ mine
    keep = (route == labels).astype(F32)
    before = lax.broadcasted_iota(jnp.int32, (count, count), 0)
    after = lax.broadcasted_iota(jnp.int32, (count, count), 1)
    rank = dot(keep.astype(BF16), (before <= after).astype(BF16)) * keep
    slot = (lax.broadcasted_iota(jnp.int32, (slots, count), 0) + 1).astype(F32)
    return jnp.concatenate([slot == rank[m : m + 1, :] for m in range(experts)]).astype(BF16)


def picks_kernel(experts, far, route_ref, mine, tokens_ref, *refs):
    outs, (route, tokens, sems) = refs[:-3], refs[-3:]
    made = [
        pltpu.make_async_copy(route_ref, route, sems.at[0]),
        pltpu.make_async_copy(tokens_ref.at[0], tokens, sems.at[1]),
    ]
    for item in made:
        item.start()
    made[0].wait()
    picks, outs = outs[: route.shape[0]], outs[route.shape[0] :]
    hot = None
    for index, out in enumerate(picks):
        value = picked(route[index : index + 1, :], mine[0], experts)
        out[...] = value
        hot = value if hot is None else hot
    made[1].wait()
    slots = hot.shape[0] // experts
    for m, out in zip(far, outs):
        out[...] = dot(hot[m * slots : (m + 1) * slots], tokens[...]).astype(BF16)


def picks_call(routing, mine, tokens, experts, far):
    rounds, count, depth = tokens.shape
    shape = jax.ShapeDtypeStruct
    slots = count // 2
    outs = [shape((experts * slots, count), BF16)] * rounds + [shape((slots, depth), BF16)] * len(far)
    result = pl.pallas_call(
        lambda *refs: picks_kernel(experts, far, *refs),
        out_shape=outs,
        in_specs=[ANY, SMEM, ANY],
        out_specs=[VMEM] * len(outs),
        scratch_shapes=[
            pltpu.VMEM((rounds, count), jnp.int32),
            pltpu.VMEM((count, depth), BF16),
            pltpu.SemaphoreType.DMA((2,)),
        ],
        compiler_params=limit(52),
        name="picks",
    )(routing, mine, tokens)
    return result[:rounds], result[rounds:]


def squeeze_kernel(count, chosen, experts, refs):
    picks, sources, outs = refs[0], refs[1 : 1 + count], refs[1 + count :]
    slots = picks.shape[0] // experts
    hot = picks[: (max(chosen) + 1) * slots, :]
    place = 0
    for source in sources:
        value = dot(hot, source[0]).astype(BF16)
        for m, out in zip(chosen, outs):
            out[:, place : place + value.shape[1]] = value[m * slots : (m + 1) * slots, :]
        place += value.shape[1]


def squeeze_call(index, picks, sources, chosen, experts):
    width = sum(item.shape[2] for item in sources)
    outs = [jax.ShapeDtypeStruct((picks.shape[0] // experts, width), BF16)] * len(chosen)

    def whole(item):
        return pl.BlockSpec(item.shape, lambda i: (0, 0))

    return pl.pallas_call(
        lambda *refs: squeeze_kernel(len(sources), chosen, experts, refs),
        grid=(1,),
        out_shape=outs,
        in_specs=[whole(picks)]
        + [pl.BlockSpec((1,) + item.shape[1:], lambda i: (index, 0, 0)) for item in sources],
        out_specs=[whole(item) for item in outs],
        compiler_params=limit(16),
        name="squeeze",
    )(picks, *sources)


def backward_kernel(sizes, where, refs):
    names = iter(refs)
    slopes, weights = grouped(names, sizes)
    outs = list(names)
    count, depth = outs[0].shape
    factor = 1.0 / math.sqrt(depth)
    shaped = take(weights, 0, depth).astype(BF16)
    for out, (array, place) in zip(outs, where):
        part = slopes[array][place * count : (place + 1) * count, :]
        out[...] = (dot_last(part, shaped) * factor).astype(BF16)


def backward_call(slopes, weights, where, count):
    depth = sum(item.shape[0] for item in weights)
    sizes = sizes_of([slopes, weights])
    return pl.pallas_call(
        lambda *refs: backward_kernel(sizes, where, refs),
        out_shape=[jax.ShapeDtypeStruct((count, depth), BF16)] * len(where),
        in_specs=[VMEM] * sum(sizes),
        out_specs=[VMEM] * len(where),
        compiler_params=limit(16),
        name="row_gradients",
    )(*slopes, *weights)


def average_call(parts, start, stop, depth, buffer):
    flat = [item for part in parts for item in part]
    sizes = sizes_of(parts)
    extra = [] if buffer is None else [buffer]
    width = flat[0].shape[1]

    def kernel(*refs):
        names = iter(refs)
        groups = grouped(names, sizes)
        out, value, sem = list(names)[len(extra) :]
        value[...] = mixed(groups, start, stop)
        made = pltpu.make_async_copy(value, out.at[pl.ds(start, stop - start), :], sem)
        made.start()
        made.wait()

    return pl.pallas_call(
        kernel,
        out_shape=jax.ShapeDtypeStruct((depth, width), F32),
        in_specs=[VMEM] * len(flat) + [ANY] * len(extra),
        out_specs=ANY,
        scratch_shapes=[pltpu.VMEM((stop - start, width), F32), pltpu.SemaphoreType.DMA(())],
        input_output_aliases={len(flat): 0} if extra else {},
        compiler_params=limit(12),
        name="average",
    )(*flat, *extra)


def finish_call(index, picks, backs, buffer):
    count, depth = picks.shape[1], backs[0].shape[1]
    extra = [] if buffer is None else [buffer]

    def kernel(*refs):
        rows = take(refs[1 : 1 + len(backs)], 0, refs[0].shape[0])
        refs[-1][0] = dot_first(refs[0][...], rows).astype(BF16)

    def whole(item):
        return pl.BlockSpec(item.shape, lambda i: (0, 0))

    return pl.pallas_call(
        kernel,
        grid=(1,),
        out_shape=jax.ShapeDtypeStruct((ROUNDS, count, depth), BF16),
        in_specs=[whole(item) for item in (picks, *backs)] + [ANY] * len(extra),
        out_specs=pl.BlockSpec((1, count, depth), lambda i: (index, 0, 0)),
        input_output_aliases={1 + len(backs): 0} if extra else {},
        compiler_params=limit(12),
        name="finish",
    )(picks, *backs, *extra)


def on_device(tokens, routing, out_grad, weights, momentum):
    experts = lax.axis_size("expert")
    weight = weights[0, 0]
    moment = momentum[0, 0]
    depth = weight.shape[0]
    _, two = split(depth)
    slots = tokens.shape[1] // 2
    mine = lax.axis_index("expert").astype(jnp.int32).reshape(1)

    def exchanged(items):
        got = [items[0]]
        for m in range(1, experts):
            got.append(swapped(items[m], "expert", m))
        return got

    in_grad = None
    waiting = []
    every, close = list(range(experts)), [0, 1]
    all_picks, items = picks_call(routing, mine, tokens, experts, every[2:])
    items = [*squeeze_call(0, all_picks[0], [tokens], close, experts), *items]
    rows = exchanged(items)
    items = squeeze_call(0, all_picks[0], [out_grad], every, experts)
    grads = exchanged(items)
    items = squeeze_call(1, all_picks[1], [tokens, out_grad], every, experts)
    later = exchanged(items)
    moment, slopes = part_call(rows[:2], grads[:2], weight, moment, 0.9)
    all_slopes = [slopes]
    (pre,) = ahead_call(rows[3:], [[weight]], depth)
    moment, slopes = part_call(rows[2:3], grads[2:3], weight, moment, 1.0)
    all_slopes.append(slopes)
    where = [
        [(0, m) if m < 2 else (min(m - 1, 2), max(m - 3, 0)) for m in range(experts)],
        [(0, m) for m in range(experts)],
    ]
    weights = [weight]
    parts = []
    for index in range(ROUNDS):
        if index:
            moment, slopes, low, rest, scale, stepped, share, late = round_call(
                later, later, depth, 0.9, pre, weights, moment, parts
            )
            weights = [*weights, late]
            all_slopes = [slopes]
        else:
            moment, slopes, low, rest, scale, stepped, share = round_call(
                rows[3:], grads[3:], 0, 1.0, pre, weights, moment, parts
            )
            all_slopes.append(slopes)
        stepped_low, ones, twos = second_call(low, rest, scale, share, weights)
        firsts = []
        for item in ones:
            firsts.append(crossed(item, "node", 2))
        seconds = []
        for item in twos:
            seconds.append(crossed(item, "node", -2))
        nears = []
        got = [firsts[0], jnp.concatenate(firsts[1:])]
        for piece, item in enumerate((share, jnp.concatenate(ones[1:]))):
            pair = (item.astype(F32) + got[piece].astype(F32)).astype(BF16)
            nears.append(swapped(pair, "node", 1))
        far = backward_call(all_slopes, weights, where[index][2:], slots)
        near = backward_call(all_slopes, weights, where[index][:2], slots)
        waiting.append(exchanged([*near, *far]))
        halves = [stepped, stepped_low]
        parts = [halves, firsts, seconds, nears]
        early_parts = [halves, firsts[:2], seconds[:1], nears[:2]]
        if index < ROUNDS - 1:
            upper, pre = ahead_call(later, early_parts, two[0])
            weights = [upper]
        else:
            for done, backs in enumerate(waiting):
                in_grad = finish_call(done, all_picks[done], backs, in_grad)
            weight = average_call(early_parts, 0, two[0], depth, None)
            weight = average_call(parts, two[0], depth, depth, weight)
    return (weight[None, None], moment[None, None], in_grad)


def solution(mesh):
    return jax.shard_map(
        on_device,
        mesh=mesh,
        in_specs=(
            P(None, ("expert", "node"), None),
            P(None, ("expert", "node")),
            P(None, ("expert", "node"), None),
            P("node", "expert", None, None),
            P("node", "expert", None, None),
        ),
        out_specs=(
            P("node", "expert", None, None),
            P("node", "expert", None, None),
            P(None, ("expert", "node"), None),
        ),
        check_vma=False,
    )
```
